512 devices in a mesh: pipe: 8 (over x, y_hi), ctx: 64 (over z, y_lo, core).
Axes of the slice: x: 4, y: 4 (y_hi: 2, y_lo: 2; y = y_hi * 2 + y_lo), z: 16, core: 2. Of those that a mesh axis runs over, the one named last changes fastest.
Arguments:
- saved_in: bfloat16 [8, 8192, 2048], P('pipe', 'ctx'), may hold values from -20 to 20, as said below
- grad_in: bfloat16 [8, 8192, 2048], P('pipe', 'ctx'), may hold values from -6 to 6
- queries: bfloat16 [8, 8192, 2048], P('pipe', 'ctx'), may hold values from -60 to 60
- d_heads: bfloat16 [8, 8192, 2048], P('pipe', 'ctx'), may hold values from -6 to 6
- kv_weights: bfloat16 [8, 2048, 512], P('pipe', 'ctx'), may hold values from -0.125 to 0.125
Outputs:
- grad_out: bfloat16 [8, 8192, 2048], P('pipe', 'ctx')
- d_queries: bfloat16 [8, 8192, 2048], P('pipe', 'ctx')
- weight_grad: float32 [8, 2048, 512], P('pipe', 'ctx')
The draws below stay inside these ranges and needn't reach their ends.
Inputs may be any that keep to these rules, and one draw needn't show every extreme that they name: `saved_in`: stored layer activations.
All inputs are finite; a program needn't handle non-finite values.
Results may differ from the reference program's by a relative error of at most 0.0039.
The reference program's roundings to bfloat16 on the way count: a program that leaves them out, or rounds other values in their place, can miss the bound.
Values may be sent and summed in bfloat16 or wider, within the bound.
A program may use at most 64 MiB of HBM per device.

```python
import math
import jax
import jax.numpy as jnp
from jax import lax

D = 2048
HEADS = 16
HEAD_DIM = 128
KV_HEADS = 2
TOK_DEV = 128
KV_WIDTH = 256
SECTIONS = 8
TOKENS = 8192
N_CTX = 64


def draw_saved_in(key, part):
    shape = (SECTIONS, TOKENS, D)
    base_key = jax.random.fold_in(jax.random.fold_in(key, 11), 0)
    return jnp.clip(jax.random.normal(base_key, shape, jnp.float32), -4.0, 4.0).astype(jnp.bfloat16)


def draw_queries(key, part):
    shape = (SECTIONS, TOKENS, D)
    base_key = jax.random.fold_in(jax.random.fold_in(key, 23), 0)
    values = jnp.clip(jax.random.normal(base_key, shape, jnp.float32), -4.0, 4.0)
    return values.astype(jnp.bfloat16)


def block_levels(stream_key, dims, cuts, least, largest):
    loudness = 1.0
    for dim, blocks in cuts:
        steps = jax.random.uniform(jax.random.fold_in(jax.random.fold_in(stream_key, 6), dim), (blocks,), jnp.float32, least / len(cuts), largest / len(cuts))
        loudness = loudness * jnp.repeat(jnp.exp(steps), dims[dim] // blocks).reshape((-1,) + (1,) * (len(dims) - 1 - dim))
    return loudness


def gaussian(key, shape, width, most, pieces=(), dtype=jnp.bfloat16):
    result = jax.random.normal(key, shape, jnp.float32) * width
    if len(pieces) > 0:
        result = block_levels(key, shape, pieces, -0.22, 0.18) * result
    return jnp.clip(result, min=-most, max=most).astype(dtype)


def setup_inputs(seed: int = 0) -> dict:
    key_of = jax.random.split(jax.random.key(seed), 6)
    saved_in = draw_saved_in(jax.random.fold_in(key_of[5], 71), 0)
    grad_in = gaussian(key_of[1], (SECTIONS, TOKENS, D), 1.0, 6.0, ((0, 8), (1, 64)))
    queries = draw_queries(jax.random.fold_in(key_of[5], 71), 0)
    d_heads = gaussian(key_of[3], (SECTIONS, TOKENS, D), 1.0, 6.0, ((0, 8), (1, 64)))
    kv_weights = gaussian(key_of[4], (SECTIONS, D, 2 * KV_WIDTH), D ** -0.5, 0.125, ((0, 8), (1, 64)))
    return {"saved_in": saved_in, "grad_in": grad_in, "queries": queries, "d_heads": d_heads, "kv_weights": kv_weights}


epsilon = 1e-06

def neighbours(blocks):
    return jnp.concatenate([jnp.roll(blocks, 1, axis=0), blocks, jnp.roll(blocks, -1, axis=0)], axis=1)

def fold_back(wide_rows):
    lower = wide_rows[:, :TOK_DEV]
    middle = wide_rows[:, TOK_DEV:2 * TOK_DEV]
    upper = wide_rows[:, 2 * TOK_DEV:]
    return middle + jnp.roll(lower, -1, axis=0) + jnp.roll(upper, 1, axis=0)

def window_mask(row_count):
    query_pos = lax.broadcasted_iota(jnp.int32, (row_count, 3 * row_count), 0)
    key_pos = lax.broadcasted_iota(jnp.int32, (row_count, 3 * row_count), 1)
    offset = key_pos - query_pos
    return (offset >= 0) & (offset <= 2 * row_count)

def section_pass(saved, upstream, query_in, grad_heads, kv_matrix):
    per_group = HEADS // KV_HEADS
    score_scale = 1.0 / math.sqrt(HEAD_DIM)
    highest = lax.Precision.HIGHEST
    blocks = saved.reshape(N_CTX, TOK_DEV, D).astype(jnp.float32)
    factor = lax.rsqrt(lax.optimization_barrier(jnp.mean(blocks * blocks, axis=-1, keepdims=True)) + epsilon)
    normed = blocks * factor
    normed_b = normed.astype(jnp.bfloat16)
    flat_b = normed_b.reshape(TOKENS, D)
    kv_rows = jnp.dot(flat_b, kv_matrix, preferred_element_type=jnp.float32).astype(jnp.bfloat16)
    kv_rows = kv_rows.reshape(N_CTX, TOK_DEV, 2 * KV_WIDTH)
    key_rows = neighbours(kv_rows[..., :KV_WIDTH]).reshape(N_CTX, 3 * TOK_DEV, KV_HEADS, HEAD_DIM).astype(jnp.float32)
    value_rows = neighbours(kv_rows[..., KV_WIDTH:]).reshape(N_CTX, 3 * TOK_DEV, KV_HEADS, HEAD_DIM).astype(jnp.float32)
    query_rows = query_in.reshape(N_CTX, TOK_DEV, KV_HEADS, per_group, HEAD_DIM).astype(jnp.float32)
    grad_rows = grad_heads.reshape(N_CTX, TOK_DEV, KV_HEADS, per_group, HEAD_DIM).astype(jnp.float32)
    scores = jnp.einsum('bqgne,bkge->bgnqk', query_rows, key_rows) * score_scale
    scores = jnp.where(window_mask(TOK_DEV)[None, None, None], scores, -1e+30)
    row_peak = lax.optimization_barrier(jnp.max(scores, axis=-1, keepdims=True))
    lifted = jnp.exp(scores - row_peak)
    probs = lifted / lax.optimization_barrier(jnp.sum(lifted, axis=-1, keepdims=True))
    probs_b = probs.astype(jnp.bfloat16).astype(jnp.float32)
    d_probs = jnp.einsum('bqgne,bkge->bgnqk', grad_rows, value_rows)
    row_dot = lax.optimization_barrier(jnp.sum(probs * d_probs, axis=-1, keepdims=True))
    d_scores = (probs * (d_probs - row_dot) * score_scale).astype(jnp.bfloat16).astype(jnp.float32)
    d_queries = jnp.einsum('bgnqk,bkge->bqgne', d_scores, key_rows).astype(jnp.bfloat16).reshape(TOKENS, D)
    d_key_wide = jnp.einsum('bgnqk,bqgne->bkge', d_scores, query_rows).reshape(N_CTX, 3 * TOK_DEV, KV_WIDTH)
    d_value_wide = jnp.einsum('bgnqk,bqgne->bkge', probs_b, grad_rows).reshape(N_CTX, 3 * TOK_DEV, KV_WIDTH)
    d_kv = jnp.concatenate([fold_back(d_key_wide), fold_back(d_value_wide)], axis=-1).reshape(TOKENS, 2 * KV_WIDTH)
    d_normed = jnp.dot(d_kv, kv_matrix.astype(jnp.float32).T, precision=highest).reshape(N_CTX, TOK_DEV, D)
    upstream_wide = upstream.reshape(N_CTX, TOK_DEV, D).astype(jnp.float32)
    grad_out = (upstream_wide + factor * (d_normed - normed * lax.optimization_barrier(jnp.mean(d_normed * normed, axis=-1, keepdims=True)))).astype(jnp.bfloat16)
    weight_grad = jnp.dot(flat_b.astype(jnp.float32).T, d_kv, precision=highest) * (1.0 / math.sqrt(TOKENS))
    return (grad_out.reshape(TOKENS, D), d_queries, weight_grad)

def reference(saved_in, grad_in, queries, d_heads, kv_weights):
    grad_outs = []
    query_grads = []
    weight_grads = []
    for section in range(SECTIONS):
        upstream = grad_in[(section + 1) % SECTIONS]
        grad_out, d_queries, weight_grad = section_pass(saved_in[section], upstream, queries[section], d_heads[section], kv_weights[section])
        grad_outs.append(grad_out)
        query_grads.append(d_queries)
        weight_grads.append(weight_grad)
    return (jnp.stack(grad_outs), jnp.stack(query_grads), jnp.stack(weight_grads))
```

```python
import functools
import math

import jax
import jax.numpy as jnp
from jax import lax
from jax.experimental import pallas as pl
from jax.experimental.pallas import tpu as pltpu
from jax.sharding import PartitionSpec as P

HEADS = 16
HEAD_DIM = 128
KV_HEADS = 2
PER_GROUP = HEADS // KV_HEADS
LANES = 4
EPSILON = 1e-06

F32 = jnp.float32
BF16 = jnp.bfloat16
NT = (((1,), (1,)), ((), ()))


def dot(a, b, dims=(((1,), (0,)), ((), ()))):
    return lax.dot_general(a, b, dims, preferred_element_type=F32)


def kernel(
    n_pipe, n_ctx,
    z_ref, up_ref, q_ref, g_ref, w_ref,
    go_ref, dq_ref, wg_ref,
    z_v, q_v, g_v, up_v, go_v, dq_v, wg_v,
    nb, fac, nt, nt_sh, w_v, kvw, acc,
    dkw, fold, dkv_hi, dkv_lo, dkv_sh, prod, dn, dot_sum,
    p_snd, p_rcv, m_snd, m_rcv,
    loc_sem, out_sem,
    ag_recv, ag_zp, ag_zm, ag_y, ag_c, ag_yc,
    nt_snd, nt_rcv, up_snd, up_rcv,
    halo_snd, halo_rcv, fold_snd, fold_rcv,
    sh_snd, sh_rcv, shf_snd,
    ps_snd, ps_rcv, ms_snd, ms_rcv,
):
    rows = z_v.shape[0]
    zs = n_ctx // LANES
    hp = zs // 2
    hm = zs - 1 - hp
    feats = w_ref.shape[0]
    width = LANES * feats
    scale = 1.0 / math.sqrt(HEAD_DIM)

    pipe = lax.axis_index("pipe")
    ctx = lax.axis_index("ctx")
    z = ctx // LANES
    lane = lax.rem(ctx, LANES)
    y = lane // 2
    core = lax.rem(lane, 2)
    lane_c = 2 * y + (1 - core)
    lane_y = 2 * (1 - y) + core
    lane_d = 2 * (1 - y) + (1 - core)

    def at_z(distance):
        return lax.rem(z + distance + zs, zs)

    def dev(zz, ll):
        return zz * LANES + ll

    z_next, z_prev = dev(at_z(1), lane), dev(at_z(-1), lane)
    me_c, me_y, me_d = dev(z, lane_c), dev(z, lane_y), dev(z, lane_d)
    right = lax.rem(ctx + 1, n_ctx)
    left = lax.rem(ctx + n_ctx - 1, n_ctx)
    pipe_prev = lax.rem(pipe + n_pipe - 1, n_pipe)
    pipe_next = lax.rem(pipe + 1, n_pipe)

    def remote(src, dst, snd, rcv, to, to_pipe=None):
        return pltpu.make_async_remote_copy(
            src_ref=src, dst_ref=dst, send_sem=snd, recv_sem=rcv,
            device_id=(pipe if to_pipe is None else to_pipe, to),
            device_id_type=pl.DeviceIdType.MESH,
        )

    loads = [
        pltpu.make_async_copy(z_ref, z_v, loc_sem.at[0]),
        pltpu.make_async_copy(
            w_ref, w_v.at[pl.ds(pl.multiple_of(ctx * feats, feats), feats)], loc_sem.at[1]
        ),
        pltpu.make_async_copy(q_ref, q_v, loc_sem.at[2]),
        pltpu.make_async_copy(g_ref, g_v, loc_sem.at[3]),
    ]
    for load in loads:
        load.start()

    barrier = pltpu.get_barrier_semaphore()
    greeted = [(pipe, d) for d in (z_next, z_prev, me_c, me_y, me_d, right, left)]
    if n_pipe > 1:
        greeted += [(pipe_prev, ctx), (pipe_next, ctx)]
    for who in greeted:
        pl.semaphore_signal(barrier, inc=1, device_id=who, device_id_type=pl.DeviceIdType.MESH)
    pl.semaphore_wait(barrier, len(greeted))

    def piece_at(zz, ll):
        start = pl.multiple_of((zz * LANES + ll) * feats, feats)
        return w_v.at[pl.ds(start, feats)], ag_recv.at[zz * LANES + ll]

    def push(zz, ll, to, snd, own=False):
        dst, rcv = piece_at(zz, ll)
        return remote(w_ref if own else dst, dst, snd.at[zz], rcv, to)

    def arrive(zz, ll):
        dst, rcv = piece_at(zz, ll)
        remote(dst, dst, ag_yc.at[zz], rcv, me_c).wait_recv()

    pushes = []

    def start(copy):
        copy.start()
        pushes.append(copy)

    start(push(z, lane, z_next, ag_zp, own=True))
    if hm > 0:
        start(push(z, lane, z_prev, ag_zm, own=True))
    start(push(z, lane, me_y, ag_y, own=True))
    start(push(z, lane, me_c, ag_c, own=True))

    loads[0].wait()
    z_wide = z_v[...].astype(F32)
    factor = lax.rsqrt(jnp.mean(z_wide * z_wide, axis=-1, keepdims=True) + EPSILON)
    fac[...] = jnp.broadcast_to(factor, fac.shape)
    nb[...] = (z_wide * factor).astype(BF16)
    for k in range(zs):
        block = nb[:, k * width:(k + 1) * width].astype(F32)
        nt[k] = block.T.astype(BF16).reshape(LANES, feats, rows)

    for i, (ll, to) in enumerate(((lane_c, me_c), (lane_y, me_y), (lane_d, me_d))):
        start(remote(nt.at[:, ll], nt_sh.at[lane], nt_snd.at[i], nt_rcv.at[lane], to))
    nt_sh[lane] = nt[:, lane]
    loads[1].wait()
    acc[...] = jnp.zeros_like(acc)

    def project(zz):
        at = pl.multiple_of(zz * width, width)
        acc[...] += dot(nb[:, pl.ds(at, width)], w_v[pl.ds(at, width), :])

    def slices(s):
        if s == 0:
            return [z]
        return ([at_z(-s)] if s <= hp else []) + ([at_z(s)] if s <= hm else [])

    for s in range(1, hp + 3):
        if s <= hp:
            zz = at_z(-s)
            arrive(zz, lane)
            if s < hp:
                start(push(zz, lane, z_next, ag_zp))
            start(push(zz, lane, me_y, ag_y))
            start(push(zz, lane, me_c, ag_c))
        if s <= hm:
            zz = at_z(s)
            arrive(zz, lane)
            if s < hm:
                start(push(zz, lane, z_prev, ag_zm))
            start(push(zz, lane, me_y, ag_y))
            start(push(zz, lane, me_c, ag_c))
        if 1 <= s <= hp + 1:
            for zz in slices(s - 1):
                arrive(zz, lane_y)
                start(push(zz, lane_y, me_c, ag_yc))
        if s >= 2:
            for zz in slices(s - 2):
                arrive(zz, lane_c)
                arrive(zz, lane_d)
                project(zz)

    kvw[1] = acc[...].astype(BF16)
    to_right = remote(kvw.at[1], kvw.at[0], halo_snd.at[0], halo_rcv.at[0], right)
    to_left = remote(kvw.at[1], kvw.at[2], halo_snd.at[1], halo_rcv.at[1], left)
    start(to_right)
    start(to_left)
    if n_pipe > 1:
        shift = remote(up_ref, up_v, up_snd, up_rcv, ctx, pipe_prev)
        start(shift)
    else:
        shift = pltpu.make_async_copy(up_ref, up_v, up_rcv)
        shift.start()
    loads[2].wait()
    loads[3].wait()
    to_right.wait_recv()
    to_left.wait_recv()

    key_pos = lax.broadcasted_iota(jnp.int32, (rows, rows), 0)
    query_pos = lax.broadcasted_iota(jnp.int32, (rows, rows), 1)
    lower = key_pos >= query_pos
    upper = key_pos <= query_pos

    def attention(group, first, last):
        def pair(i, carry):
            keys = kvw[:, :, group * HEAD_DIM:(group + 1) * HEAD_DIM].reshape(3 * rows, HEAD_DIM)
            at_v = (KV_HEADS + group) * HEAD_DIM
            values = kvw[:, :, at_v:at_v + HEAD_DIM].reshape(3 * rows, HEAD_DIM)
            made = []
            for j in range(2):
                at = pl.multiple_of((group * PER_GROUP + 2 * i + j) * HEAD_DIM, HEAD_DIM)
                query = q_v[:, pl.ds(at, HEAD_DIM)]
                grad = g_v[:, pl.ds(at, HEAD_DIM)]
                scores = dot(keys, query, NT) * scale
                scores = jnp.concatenate(
                    [
                        jnp.where(lower, scores[:rows], -1e30),
                        scores[rows:2 * rows],
                        jnp.where(upper, scores[2 * rows:], -1e30),
                    ],
                    axis=0,
                )
                peak = jnp.max(scores, axis=0, keepdims=True)
                lifted = jnp.exp(scores - peak)
                probs = lifted * (1.0 / jnp.sum(lifted, axis=0, keepdims=True))
                d_probs = dot(values, grad, NT)
                row_dot = jnp.sum(probs * d_probs, axis=0, keepdims=True)
                d_scores = (probs * (d_probs - row_dot) * scale).astype(BF16)
                d_query = dot(d_scores, keys, (((0,), (0,)), ((), ())))
                dq_v[:, pl.ds(at, HEAD_DIM)] = d_query.astype(BF16)
                made.append((d_scores, probs.astype(BF16), query, grad))
            d_keys = dot(
                jnp.concatenate([made[0][0], made[1][0]], axis=1),
                jnp.concatenate([made[0][2], made[1][2]], axis=0),
            )
            d_values = dot(
                jnp.concatenate([made[0][1], made[1][1]], axis=1),
                jnp.concatenate([made[0][3], made[1][3]], axis=0),
            )
            dkw[group, :, :HEAD_DIM] += d_keys
            dkw[group, :, HEAD_DIM:] += d_values
            return carry

        lax.fori_loop(first, last, pair, 0)

    def fold_copies(group):
        return (
            remote(dkw.at[group, pl.ds(2 * rows, rows)], fold.at[0, group],
                   fold_snd.at[0, group], fold_rcv.at[0, group], right),
            remote(dkw.at[group, pl.ds(0, rows)], fold.at[1, group],
                   fold_snd.at[1, group], fold_rcv.at[1, group], left),
        )

    def fold_start(group):
        for copy in fold_copies(group):
            start(copy)

    def share_start(group):
        for copy in fold_copies(group):
            copy.wait_recv()
        total = dkw[group, rows:2 * rows] + fold[0, group] + fold[1, group]
        high = total.astype(BF16)
        low = (total - high.astype(F32)).astype(BF16)
        dkv_sh[lane, group] = high
        at_k, at_v = group * HEAD_DIM, (KV_HEADS + group) * HEAD_DIM
        for into, part in ((dkv_hi, high), (dkv_lo, low)):
            into[:, at_k:at_k + HEAD_DIM] = part[:, :HEAD_DIM]
            into[:, at_v:at_v + HEAD_DIM] = part[:, HEAD_DIM:]
        own = dkv_sh.at[lane, group]
        start(remote(own, own, sh_snd.at[0, group], sh_rcv.at[group, lane], me_y))
        start(remote(own, own, sh_snd.at[1, group], sh_rcv.at[group, lane], me_c))

    def shared(group, ll, snd):
        part = dkv_sh.at[ll, group]
        return remote(part, part, snd, sh_rcv.at[group, ll], me_c)

    def share_pass(group):
        passed = shared(group, lane_y, shf_snd.at[group])
        passed.wait_recv()
        start(passed)

    def ring_copy(group, step, plus):
        snd, rcv = (p_snd, p_rcv) if plus else (m_snd, m_rcv)
        s_sem, r_sem = (ps_snd, ps_rcv) if plus else (ms_snd, ms_rcv)
        return remote(
            snd.at[group, step - 1], rcv.at[group, step - 1],
            s_sem.at[group, step - 1], r_sem.at[group, step - 1],
            z_next if plus else z_prev,
        )

    def ring_start(group):
        for ll in (lane_c, lane_d):
            shared(group, ll, shf_snd.at[group]).wait_recv()
        held = jnp.concatenate(
            [nt_sh[p].reshape(zs * feats, rows) for p in range(LANES)], axis=1
        )
        terms = dot(held, dkv_sh[:, group].reshape(LANES * rows, 2 * HEAD_DIM))
        prod[group] = terms.reshape(zs, feats, 2 * HEAD_DIM)
        p_snd[group, 0] = prod[group, at_z(hp)]
        start(ring_copy(group, 1, True))
        if hm > 0:
            m_snd[group, 0] = prod[group, at_z(-hm)]
            start(ring_copy(group, 1, False))

    def ring_step(group, step):
        ring_copy(group, step, True).wait_recv()
        if step < hp:
            p_snd[group, step] = p_rcv[group, step - 1] + prod[group, at_z(hp - step)]
            start(ring_copy(group, step + 1, True))
        if step <= hm:
            ring_copy(group, step, False).wait_recv()
            if step < hm:
                m_snd[group, step] = m_rcv[group, step - 1] + prod[group, at_z(step - hm)]
                start(ring_copy(group, step + 1, False))
        if step == hp:
            total = prod[group, z] + p_rcv[group, hp - 1]
            if hm > 0:
                total = total + m_rcv[group, hm - 1]
            total = total * (1.0 / math.sqrt(rows * n_ctx))
            at_k, at_v = group * HEAD_DIM, (KV_HEADS + group) * HEAD_DIM
            wg_v[:, at_k:at_k + HEAD_DIM] = total[:, :HEAD_DIM]
            wg_v[:, at_v:at_v + HEAD_DIM] = total[:, HEAD_DIM:]

    pairs = PER_GROUP // 2
    dkw[...] = jnp.zeros_like(dkw)
    attention(0, 0, pairs)
    fold_start(0)
    attention(1, 0, pairs // 2)
    share_start(0)
    attention(1, pairs // 2, pairs)
    fold_start(1)
    store_q = pltpu.make_async_copy(dq_v, dq_ref, out_sem.at[0])
    store_q.start()
    share_pass(0)
    for ll, to in ((lane_c, me_c), (lane_y, me_y), (lane_d, me_d)):
        remote(nt_sh.at[ll], nt_sh.at[ll], nt_snd.at[0], nt_rcv.at[ll], to).wait_recv()
    ring_start(0)
    share_start(1)
    share_pass(1)
    ring_start(1)

    model = z_v.shape[1]
    blocks = 8
    span = model // blocks
    dot_sum[...] = jnp.zeros_like(dot_sum)

    def spread(b):
        w_b = w_v[b * span:(b + 1) * span, :]
        d_b = dot(dkv_hi[...], w_b, NT) + dot(dkv_lo[...], w_b, NT)
        dn[:, b * span:(b + 1) * span] = d_b
        normed = z_v[:, b * span:(b + 1) * span].astype(F32) * fac[:, :1]
        part = d_b * normed
        total = part[:, :128]
        for k in range(1, span // 128):
            total = total + part[:, k * 128:(k + 1) * 128]
        dot_sum[...] += total

    def finish(b, mean):
        at = slice(b * span, (b + 1) * span)
        normed = z_v[:, at].astype(F32) * fac[:, :1]
        branch = fac[:, :1] * (dn[:, at] - normed * mean)
        go_v[:, at] = (up_v[:, at].astype(F32) + branch).astype(BF16)

    todo = [functools.partial(spread, b) for b in range(blocks)]

    def last():
        if n_pipe > 1:
            shift.wait_recv()
        else:
            shift.wait()
        mean = jnp.sum(dot_sum[...], axis=-1, keepdims=True) * (1.0 / model)
        for b in range(blocks):
            finish(b, mean)
        pltpu.make_async_copy(go_v, go_ref, out_sem.at[1]).start()

    todo.append(last)
    each = -(-len(todo) // max(1, hp - 1))
    for step in range(1, hp + 1):
        for group in range(KV_HEADS):
            ring_step(group, step)
        for _ in range(each):
            if todo:
                todo.pop(0)()
    while todo:
        todo.pop(0)()

    store_w = pltpu.make_async_copy(wg_v, wg_ref, out_sem.at[2])
    store_w.start()
    for copy in pushes:
        copy.wait_send()
    store_q.wait()
    pltpu.make_async_copy(go_v, go_ref, out_sem.at[1]).wait()
    store_w.wait()


def per_device(n_pipe, n_ctx, saved_in, grad_in, queries, d_heads, kv_weights):
    rows, model = saved_in.shape[1:]
    feats, kv_all = kv_weights.shape[1:]
    zs = n_ctx // LANES
    hp = zs // 2
    hm = max(1, zs - 1 - hp)
    pair = 2 * HEAD_DIM
    vm = pltpu.VMEM
    dma = pltpu.SemaphoreType.DMA
    big = vm((rows, model), BF16)
    scratch = [
        big, big, big, big, big, big, vm((feats, kv_all), F32),
        big, vm((rows, 128), F32),
        vm((zs, LANES, feats, rows), BF16), vm((LANES, zs, feats, rows), BF16),
        vm((n_ctx * feats, kv_all), BF16), vm((3, rows, kv_all), BF16), vm((rows, kv_all), F32),
        vm((KV_HEADS, 3 * rows, pair), F32), vm((2, KV_HEADS, rows, pair), F32),
        vm((rows, kv_all), BF16), vm((rows, kv_all), BF16),
        vm((LANES, KV_HEADS, rows, pair), BF16), vm((KV_HEADS, zs, feats, pair), F32),
        vm((rows, model), F32), vm((rows, 128), F32),
        vm((KV_HEADS, hp, feats, pair), F32), vm((KV_HEADS, hp, feats, pair), F32),
        vm((KV_HEADS, hm, feats, pair), F32), vm((KV_HEADS, hm, feats, pair), F32),
        dma((4,)), dma((3,)),
        dma((n_ctx,)), dma((zs,)), dma((zs,)), dma((zs,)), dma((zs,)), dma((zs,)),
        dma((3,)), dma((LANES,)), dma, dma,
        dma((2,)), dma((2,)), dma((2, KV_HEADS)), dma((2, KV_HEADS)),
        dma((2, KV_HEADS)), dma((KV_HEADS, LANES)), dma((KV_HEADS,)),
        dma((KV_HEADS, hp)), dma((KV_HEADS, hp)), dma((KV_HEADS, hm)), dma((KV_HEADS, hm)),
    ]
    any_space = pl.BlockSpec(memory_space=pl.ANY)
    grad_out, d_queries, weight_grad = pl.pallas_call(
        functools.partial(kernel, n_pipe, n_ctx),
        out_shape=(
            jax.ShapeDtypeStruct((rows, model), BF16),
            jax.ShapeDtypeStruct((rows, model), BF16),
            jax.ShapeDtypeStruct((feats, kv_all), F32),
        ),
        in_specs=[any_space] * 5,
        out_specs=(any_space,) * 3,
        scratch_shapes=scratch,
        compiler_params=pltpu.CompilerParams(
            collective_id=0, has_side_effects=True, vmem_limit_bytes=48 * 1024 * 1024
        ),
        name="step",
    )(saved_in[0], grad_in[0], queries[0], d_heads[0], kv_weights[0])
    return grad_out[None], d_queries[None], weight_grad[None]


def solution(mesh):
    spec = P("pipe", "ctx", None)
    return jax.shard_map(
        functools.partial(per_device, mesh.shape["pipe"], mesh.shape["ctx"]),
        mesh=mesh, in_specs=(spec,) * 5, out_specs=(spec,) * 3, check_vma=False,
    )
```

```python
import functools
import math

import jax
import jax.numpy as jnp
from jax import lax
from jax.experimental import pallas as pl
from jax.experimental.pallas import tpu as pltpu
from jax.sharding import PartitionSpec as P

HEADS = 16
HEAD_DIM = 128
KV_HEADS = 2
PER_GROUP = HEADS // KV_HEADS
LANES = 4
REACH = 4
EPSILON = 1e-06

F32 = jnp.float32
BF16 = jnp.bfloat16
NT = (((1,), (1,)), ((), ()))


def dot(a, b, dims=(((1,), (0,)), ((), ()))):
    return lax.dot_general(a, b, dims, preferred_element_type=F32)


def kernel(
    n_pipe, n_ctx,
    z_ref, up_ref, q_ref, g_ref, w_ref,
    go_v, dq_v, wg_v,
    z_v, q_v, g_v, up_v,
    nb, fac, nt, nt_sh, w_v, kvw, acc,
    dkw, fold, dkv_hi, dkv_lo, dkv_sh, prod, dn, dot_sum,
    p_snd, p_rcv, m_snd, m_rcv,
    loc_sem, ag_snd, ag_z, ag_y, ag_c,
    nt_snd, nt_rcv, up_snd, up_rcv,
    halo_snd, halo_rcv, fold_snd, fold_rcv,
    sh_snd, sh_rcv,
    p_sent, p_came, m_sent, m_came,
):
    rows = z_v.shape[0]
    zs = n_ctx // LANES
    hp = zs // 2
    hm = zs - 1 - hp
    feats = w_ref.shape[0]
    width = LANES * feats
    scale = 1.0 / math.sqrt(HEAD_DIM)

    pipe = lax.axis_index("pipe")
    ctx = lax.axis_index("ctx")
    z = ctx // LANES
    lane = lax.rem(ctx, LANES)
    y = lane // 2
    core = lax.rem(lane, 2)
    lane_c = 2 * y + (1 - core)
    lane_y = 2 * (1 - y) + core
    lane_d = 2 * (1 - y) + (1 - core)

    def at_z(distance):
        return lax.rem(z + distance + zs, zs)

    def dev(zz, ll):
        return zz * LANES + ll

    ups = [dev(at_z(k), lane) for k in range(1, min(max(2, REACH), hp) + 1)]
    downs = [dev(at_z(-k), lane) for k in range(1, min(max(2, REACH), hp) + 1)]
    me_c, me_y, me_d = dev(z, lane_c), dev(z, lane_y), dev(z, lane_d)
    right = lax.rem(ctx + 1, n_ctx)
    left = lax.rem(ctx + n_ctx - 1, n_ctx)
    pipe_prev = lax.rem(pipe + n_pipe - 1, n_pipe)
    pipe_next = lax.rem(pipe + 1, n_pipe)

    def remote(src, dst, snd, rcv, to, to_pipe=None):
        return pltpu.make_async_remote_copy(
            src_ref=src, dst_ref=dst, send_sem=snd, recv_sem=rcv,
            device_id=(pipe if to_pipe is None else to_pipe, to),
            device_id_type=pl.DeviceIdType.MESH,
        )

    loads = [
        pltpu.make_async_copy(z_ref, z_v, loc_sem.at[0]),
        pltpu.make_async_copy(
            w_ref, w_v.at[pl.ds(pl.multiple_of(ctx * feats, feats), feats)], loc_sem.at[1]
        ),
        pltpu.make_async_copy(q_ref, q_v, loc_sem.at[2]),
        pltpu.make_async_copy(g_ref, g_v, loc_sem.at[3]),
    ]
    for load in loads:
        load.start()

    with jax.named_scope("greet"):
        barrier = pltpu.get_barrier_semaphore()
        greeted = [(pipe, d) for d in (*ups, *downs, me_c, me_y, me_d, right, left)]
        if n_pipe > 1:
            greeted += [(pipe_prev, ctx), (pipe_next, ctx)]
        for who in greeted:
            pl.semaphore_signal(barrier, inc=1, device_id=who, device_id_type=pl.DeviceIdType.MESH)
        pl.semaphore_wait(barrier, len(greeted))

    def piece_at(zz, ll):
        return w_v.at[pl.ds(pl.multiple_of((zz * LANES + ll) * feats, feats), feats)]

    def pieces(count):
        return w_v.at[pl.ds(0, count * feats)]

    sent = [0]

    def push(zz, ll, to, came, own=False):
        sent[0] += 1
        remote(w_ref if own else piece_at(zz, ll), piece_at(zz, ll), ag_snd, came, to).start()

    def arrive(count, came):
        remote(pieces(count), pieces(count), ag_snd, came, me_c).wait_recv()

    early = rows // 2

    def shift(part):
        at = pl.ds(0, early) if part == 0 else pl.ds(early, rows - early)
        if n_pipe > 1:
            return remote(up_ref.at[at], up_v.at[at], up_snd, up_rcv, ctx, pipe_prev)
        return pltpu.make_async_copy(up_ref.at[at], up_v.at[at], up_rcv)

    def chain(distance, upward):
        reach, to = (hp, ups) if upward else (hm, downs)
        zz = at_z(-distance if upward else distance)
        for stride in (1, 2) if distance == 0 else (2,):
            if distance + stride <= reach:
                push(zz, lane, to[stride - 1], ag_z.at[int(upward), distance + stride - 1], own=distance == 0)

    chain(0, True)
    chain(0, False)
    push(z, lane, me_y, ag_y.at[0], own=True)
    push(z, lane, me_c, ag_c.at[0], own=True)

    with jax.named_scope("norm"):
        loads[0].wait()
        z_wide = z_v[...].astype(F32)
        factor = lax.rsqrt(jnp.mean(z_wide * z_wide, axis=-1, keepdims=True) + EPSILON)
        fac[...] = jnp.broadcast_to(factor, fac.shape)
        nb[...] = (z_wide * factor).astype(BF16)
        for k in range(zs):
            block = nb[:, k * width:(k + 1) * width].astype(F32)
            nt[k] = block.T.astype(BF16).reshape(LANES, feats, rows)

    shift(0).start()
    nt_sh[lane] = nt[:, lane]
    loads[1].wait()
    acc[...] = jnp.zeros_like(acc)

    def project(zz):
        at = pl.multiple_of(zz * width, width)
        acc[...] += dot(nb[:, pl.ds(at, width)], w_v[pl.ds(at, width), :])

    def slices(s):
        if s == 0:
            return [z]
        return ([at_z(-s)] if s <= hp else []) + ([at_z(s)] if s <= hm else [])

    y_lag, c_lag = 3, 5

    def cross(s):
        found = slices(s)
        arrive(len(found), ag_y.at[s])
        for zz in found:
            push(zz, lane_y, me_c, ag_c.at[s])

    for s in range(1, hp + c_lag + 1):
        with jax.named_scope(f"ag{s}"):
            if s <= hp:
                for zz, upward in zip(slices(s), (True, False)):
                    arrive(1, ag_z.at[int(upward), s - 1])
                    chain(s, upward)
                    push(zz, lane, me_y, ag_y.at[s])
                    push(zz, lane, me_c, ag_c.at[s])
                for back in range(max(0, s - y_lag), hp + 1) if s == hp else [s - y_lag]:
                    if back >= 0:
                        cross(back)
            if s >= c_lag:
                found = slices(s - c_lag)
                arrive(2 * len(found), ag_c.at[s - c_lag])
                for zz in found:
                    project(zz)

    def halo_copies(group):
        own = kvw.at[group, 1]
        return (
            remote(own, kvw.at[group, 0], halo_snd, halo_rcv.at[group], right),
            remote(own, kvw.at[group, 2], halo_snd, halo_rcv.at[group], left),
        )

    for group in range(KV_HEADS):
        at_k, at_v = group * HEAD_DIM, (KV_HEADS + group) * HEAD_DIM
        kvw[group, 1, 0] = acc[:, at_k:at_k + HEAD_DIM].astype(BF16)
        kvw[group, 1, 1] = acc[:, at_v:at_v + HEAD_DIM].astype(BF16)
        for copy in halo_copies(group):
            copy.start()
    loads[2].wait()
    loads[3].wait()

    def halo_wait(group):
        both = kvw.at[group, pl.ds(0, 2)]
        remote(both, both, halo_snd, halo_rcv.at[group], right).wait_recv()

    key_pos = lax.broadcasted_iota(jnp.int32, (rows, rows), 0)
    query_pos = lax.broadcasted_iota(jnp.int32, (rows, rows), 1)
    lower = key_pos >= query_pos
    upper = key_pos <= query_pos

    def attention(group, first, count, batch):
        def some(i, carry):
            keys = kvw[group, :, 0].reshape(3 * rows, HEAD_DIM)
            values = kvw[group, :, 1].reshape(3 * rows, HEAD_DIM)
            made = []
            for j in range(batch):
                head = group * PER_GROUP + first + batch * i + j
                at = pl.multiple_of(head * HEAD_DIM, HEAD_DIM)
                query = q_v[:, pl.ds(at, HEAD_DIM)]
                grad = g_v[:, pl.ds(at, HEAD_DIM)]
                scores = dot(keys, query, NT) * scale
                scores = jnp.concatenate(
                    [
                        jnp.where(lower, scores[:rows], -1e30),
                        scores[rows:2 * rows],
                        jnp.where(upper, scores[2 * rows:], -1e30),
                    ],
                    axis=0,
                )
                peak = jnp.max(scores, axis=0, keepdims=True)
                lifted = jnp.exp(scores - peak)
                probs = lifted * (1.0 / jnp.sum(lifted, axis=0, keepdims=True))
                d_probs = dot(values, grad, NT)
                row_dot = jnp.sum(probs * d_probs, axis=0, keepdims=True)
                d_scores = (probs * (d_probs - row_dot) * scale).astype(BF16)
                d_query = dot(d_scores, keys, (((0,), (0,)), ((), ())))
                dq_v[:, pl.ds(at, HEAD_DIM)] = d_query.astype(BF16)
                made.append((d_scores, probs.astype(BF16), query, grad))
            d_scores, probs, query, grad = (tuple(m[k] for m in made) for k in range(4))
            d_keys = dot(jnp.concatenate(d_scores, axis=1), jnp.concatenate(query, axis=0))
            d_values = dot(jnp.concatenate(probs, axis=1), jnp.concatenate(grad, axis=0))
            dkw[group, :, :HEAD_DIM] += d_keys
            dkw[group, :, HEAD_DIM:] += d_values
            return carry

        lax.fori_loop(0, count // batch, some, 0)

    def fold_start(group):
        for side, start, to in ((0, 2 * rows, right), (1, 0, left)):
            remote(
                dkw.at[group, pl.ds(start, rows)], fold.at[group, side], fold_snd, fold_rcv.at[group], to
            ).start()

    def share_start(group):
        remote(fold.at[group], fold.at[group], fold_snd, fold_rcv.at[group], right).wait_recv()
        total = dkw[group, rows:2 * rows] + fold[group, 0] + fold[group, 1]
        high = total.astype(BF16)
        low = (total - high.astype(F32)).astype(BF16)
        dkv_sh[lane, group] = high
        at_k, at_v = group * HEAD_DIM, (KV_HEADS + group) * HEAD_DIM
        for into, part in ((dkv_hi, high), (dkv_lo, low)):
            into[:, at_k:at_k + HEAD_DIM] = part[:, :HEAD_DIM]
            into[:, at_v:at_v + HEAD_DIM] = part[:, HEAD_DIM:]
        share(group, lane, 0, me_y).start()
        share(group, lane, 1, me_c).start()

    def share(group, ll, kind, to):
        part = dkv_sh.at[ll, group]
        return remote(part, part, sh_snd, sh_rcv.at[group, kind], to)

    def share_pass(group):
        share(group, lane_y, 0, me_c).wait_recv()
        share(group, lane_y, 1, me_c).start()

    def ring_refs(upward):
        if upward:
            return p_snd, p_rcv, p_sent, p_came, ups, hp
        return m_snd, m_rcv, m_sent, m_came, downs, hm

    def ring_send(group, k, upward, total):
        snd, rcv, s_sem, r_sem, to, _ = ring_refs(upward)
        far = int(k > REACH)
        snd[group, k - 1] = total.astype(BF16)
        remote(
            snd.at[group, k - 1], rcv.at[group, k - 1], s_sem, r_sem.at[group, far],
            to[(k - REACH if far else k) - 1],
        ).start()

    def ring_wait(group, upward, first, count, far):
        _, rcv, s_sem, r_sem, to, _ = ring_refs(upward)
        some = rcv.at[group, pl.ds(first, count)]
        remote(some, some, s_sem, r_sem.at[group, far], to[0]).wait_recv()
        return [rcv[group, first + k].astype(F32) for k in range(count)]

    def ring_start(group):
        two = dkv_sh.at[pl.ds(0, 2), group]
        remote(two, two, sh_snd, sh_rcv.at[group, 1], me_c).wait_recv()
        held = jnp.concatenate(
            [nt_sh[p].reshape(zs * feats, rows) for p in range(LANES)], axis=1
        )
        terms = dot(held, dkv_sh[:, group].reshape(LANES * rows, 2 * HEAD_DIM))
        prod[group] = terms.reshape(zs, feats, 2 * HEAD_DIM)
        for k in range(hp, 0, -1):
            for upward, reach in ((True, hp), (False, hm)):
                if k <= reach and (k != REACH or reach <= REACH):
                    ring_send(group, k, upward, prod[group, at_z(k if upward else -k)])

    def ring_middle(group):
        for upward, reach in ((True, hp), (False, hm)):
            if reach > REACH:
                total = prod[group, at_z(REACH if upward else -REACH)]
                for term in ring_wait(group, upward, REACH, reach - REACH, 1):
                    total = total + term
                ring_send(group, REACH, upward, total)

    def ring_end(group):
        total = prod[group, z]
        for upward, reach in ((True, hp), (False, hm)):
            if reach > 0:
                for term in ring_wait(group, upward, 0, min(REACH, reach), 0):
                    total = total + term
        total = total * (1.0 / math.sqrt(rows * n_ctx))
        at_k, at_v = group * HEAD_DIM, (KV_HEADS + group) * HEAD_DIM
        wg_v[:, at_k:at_k + HEAD_DIM] = total[:, :HEAD_DIM]
        wg_v[:, at_v:at_v + HEAD_DIM] = total[:, HEAD_DIM:]

    dkw[...] = jnp.zeros_like(dkw)
    with jax.named_scope("halo0"):
        halo_wait(0)
    for ll, to in ((lane_c, me_c), (lane_y, me_y), (lane_d, me_d)):
        remote(nt.at[:, ll], nt_sh.at[lane], nt_snd, nt_rcv, to).start()
    with jax.named_scope("att0"):
        attention(0, 0, PER_GROUP, 4)
    fold_start(0)
    with jax.named_scope("halo1"):
        halo_wait(1)
    with jax.named_scope("att1a"):
        attention(1, 0, 4, 4)
        attention(1, 4, 2, 2)
    with jax.named_scope("share0"):
        share_start(0)
    with jax.named_scope("att1b"):
        attention(1, 6, 2, 2)
    fold_start(1)
    with jax.named_scope("nt"):
        three = nt_sh.at[pl.ds(0, LANES - 1)]
        remote(three, three, nt_snd, nt_rcv, me_c).wait_recv()
    with jax.named_scope("pass0"):
        share_pass(0)
    with jax.named_scope("ring0"):
        ring_start(0)
    with jax.named_scope("share1"):
        share_start(1)

    model = z_v.shape[1]
    blocks = 8
    span = model // blocks
    dot_sum[...] = jnp.zeros_like(dot_sum)

    def spread(b):
        w_b = w_v[b * span:(b + 1) * span, :]
        d_b = dot(dkv_hi[...], w_b, NT) + dot(dkv_lo[...], w_b, NT)
        dn[:, b * span:(b + 1) * span] = d_b
        normed = z_v[:, b * span:(b + 1) * span].astype(F32) * fac[:, :1]
        part = d_b * normed
        total = part[:, :128]
        for k in range(1, span // 128):
            total = total + part[:, k * 128:(k + 1) * 128]
        dot_sum[...] += total

    def finish(b, mean):
        at = slice(b * span, (b + 1) * span)
        normed = z_v[:, at].astype(F32) * fac[:, :1]
        branch = fac[:, :1] * (dn[:, at] - normed * mean)
        go_v[:, at] = (up_v[:, at].astype(F32) + branch).astype(BF16)

    todo = [functools.partial(spread, b) for b in range(blocks)]

    def last():
        with jax.named_scope("up"):
            if n_pipe > 1:
                remote(up_v, up_v, up_snd, up_rcv, ctx, pipe_prev).wait_recv()
            else:
                pltpu.make_async_copy(up_ref, up_v, up_rcv).wait()
        mean = jnp.sum(dot_sum[...], axis=-1, keepdims=True) * (1.0 / model)
        for b in range(blocks):
            finish(b, mean)

    todo.append(last)
    def fill(count):
        for _ in range(count):
            if todo:
                todo.pop(0)()

    def stage(name, act):
        with jax.named_scope(name):
            act()

    stage("fill0", lambda: fill(4))
    stage("pass1", lambda: share_pass(1))
    stage("ring1", lambda: ring_start(1))
    stage("fill1", lambda: fill(1))
    stage("mid0", lambda: ring_middle(0))
    stage("fill2", lambda: fill(3))
    shift(1).start()
    stage("mid1", lambda: ring_middle(1))
    stage("end0", lambda: ring_end(0))
    stage("last", lambda: fill(len(todo)))
    stage("end1", lambda: ring_end(1))

    with jax.named_scope("drain"):
        all_sent = [
            (pieces(sent[0]), ag_snd), (nt.at[:, pl.ds(0, LANES - 1)], nt_snd),
            (kvw.at[:, pl.ds(0, 2)], halo_snd), (fold, fold_snd),
            (dkv_sh.at[pl.ds(0, LANES - 1)], sh_snd), (p_snd, p_sent),
        ]
        if hm > 0:
            all_sent.append((m_snd, m_sent))
        if n_pipe > 1:
            all_sent.append((up_v, up_snd))
        for ref, sem in all_sent:
            remote(ref, ref, sem, sem, me_c).wait_send()


def store(go_v, dq_v, wg_v, go_ref, dq_ref, wg_ref, sem):
    copies = [
        pltpu.make_async_copy(src, dst, sem.at[i])
        for i, (src, dst) in enumerate(((go_v, go_ref), (dq_v, dq_ref), (wg_v, wg_ref)))
    ]
    for copy in copies:
        copy.start()
    for copy in copies:
        copy.wait()


def per_device(n_pipe, n_ctx, saved_in, grad_in, queries, d_heads, kv_weights):
    rows, model = saved_in.shape[1:]
    feats, kv_all = kv_weights.shape[1:]
    zs = n_ctx // LANES
    hp = zs // 2
    hm = max(1, zs - 1 - hp)
    pair = 2 * HEAD_DIM
    vm = pltpu.VMEM
    dma = pltpu.SemaphoreType.DMA
    big = vm((rows, model), BF16)
    scratch = [
        big, big, big, big,
        big, vm((rows, 128), F32),
        vm((zs, LANES, feats, rows), BF16), vm((LANES, zs, feats, rows), BF16),
        vm((n_ctx * feats, kv_all), BF16), vm((KV_HEADS, 3, 2, rows, HEAD_DIM), BF16), vm((rows, kv_all), F32),
        vm((KV_HEADS, 3 * rows, pair), F32), vm((KV_HEADS, 2, rows, pair), F32),
        vm((rows, kv_all), BF16), vm((rows, kv_all), BF16),
        vm((LANES, KV_HEADS, rows, pair), BF16), vm((KV_HEADS, zs, feats, pair), F32),
        vm((rows, model), F32), vm((rows, 128), F32),
        vm((KV_HEADS, hp, feats, pair), BF16), vm((KV_HEADS, hp, feats, pair), BF16),
        vm((KV_HEADS, hm, feats, pair), BF16), vm((KV_HEADS, hm, feats, pair), BF16),
        dma((4,)), dma, dma((2, hp)), dma((hp + 1,)), dma((hp + 1,)),
        dma, dma, dma, dma,
        dma, dma((KV_HEADS,)), dma, dma((KV_HEADS,)),
        dma, dma((KV_HEADS, 2)),
        dma, dma((KV_HEADS, 2)), dma, dma((KV_HEADS, 2)),
    ]
    hbm = pl.BlockSpec(memory_space=pltpu.HBM)
    vmem = pl.BlockSpec(memory_space=pltpu.VMEM)
    shapes = (
        jax.ShapeDtypeStruct((rows, model), BF16),
        jax.ShapeDtypeStruct((rows, model), BF16),
        jax.ShapeDtypeStruct((feats, kv_all), F32),
    )
    results = pl.pallas_call(
        functools.partial(kernel, n_pipe, n_ctx),
        out_shape=shapes,
        in_specs=[hbm] * 5,
        out_specs=(vmem,) * 3,
        scratch_shapes=scratch,
        compiler_params=pltpu.CompilerParams(
            collective_id=0, has_side_effects=True, vmem_limit_bytes=48 * 1024 * 1024
        ),
        name="step",
    )(*(
        pltpu.with_memory_space_constraint(x[0], pltpu.HBM)
        for x in (saved_in, grad_in, queries, d_heads, kv_weights)
    ))
    grad_out, d_queries, weight_grad = pl.pallas_call(
        store,
        out_shape=shapes,
        in_specs=[vmem] * 3,
        out_specs=(hbm,) * 3,
        scratch_shapes=[dma((3,))],
        name="store",
    )(*(pltpu.with_memory_space_constraint(x, pltpu.VMEM) for x in results))
    return grad_out[None], d_queries[None], weight_grad[None]


def solution(mesh):
    spec = P("pipe", "ctx", None)
    return jax.shard_map(
        functools.partial(per_device, mesh.shape["pipe"], mesh.shape["ctx"]),
        mesh=mesh, in_specs=(spec,) * 5, out_specs=(spec,) * 3, check_vma=False,
    )
```

```python
import functools
import math

import jax
import jax.numpy as jnp
from jax import lax
from jax.experimental import pallas as pl
from jax.experimental.pallas import tpu as pltpu
from jax.sharding import PartitionSpec as P

HEADS = 16
HEAD_DIM = 128
KV_HEADS = 2
PER_GROUP = HEADS // KV_HEADS
LANES = 4
REACH = 4
EPSILON = 1e-06

F32 = jnp.float32
BF16 = jnp.bfloat16
NT = (((1,), (1,)), ((), ()))


def dot(a, b, dims=(((1,), (0,)), ((), ()))):
    return lax.dot_general(a, b, dims, preferred_element_type=F32)


def over_keys(op, last, a):
    while a.shape[0] > 8:
        parts = 3 if a.shape[0] % 3 == 0 else 2
        step = a.shape[0] // parts
        total = a[:step]
        for k in range(1, parts):
            total = op(total, a[k * step:(k + 1) * step])
        a = total
    return last(a, axis=0, keepdims=True)


def kernel(
    n_pipe, n_ctx,
    z_ref, up_ref, q_ref, g_ref, w_ref,
    go_v, dq_v, wg_v,
    z_v, q_v, g_v, up_v, relay,
    nb, fac, nt, nt_sh, w_v, kvw, acc,
    dkw, folded, fold, dkv_hi, dkv_lo, dkv_sh, prod, dn, dot_sum,
    p_snd, p_rcv, m_snd, m_rcv,
    s_buf, d_buf, p_all, d_all,
    loc_sem, ag_snd, ag_z, ag_y, ag_c,
    nt_snd, nt_rcv, up_snd, up_rcv, rl_snd, rl_rcv,
    halo_snd, halo_rcv, fold_snd, fold_rcv,
    sh_snd, sh_rcv,
    p_sent, p_came, m_sent, m_came,
):
    rows = z_v.shape[0]
    zs = n_ctx // LANES
    hp = zs // 2
    hm = zs - 1 - hp
    feats = w_ref.shape[0]
    width = LANES * feats
    scale = 1.0 / math.sqrt(HEAD_DIM)

    pipe = lax.axis_index("pipe")
    ctx = lax.axis_index("ctx")
    z = ctx // LANES
    lane = lax.rem(ctx, LANES)
    y = lane // 2
    core = lax.rem(lane, 2)
    lane_c = 2 * y + (1 - core)
    lane_y = 2 * (1 - y) + core
    lane_d = 2 * (1 - y) + (1 - core)

    def at_z(distance):
        return lax.rem(z + distance + zs, zs)

    def dev(zz, ll):
        return zz * LANES + ll

    ups = [dev(at_z(k), lane) for k in range(1, min(max(4, REACH), hp) + 1)]
    downs = [dev(at_z(-k), lane) for k in range(1, min(max(4, REACH), hp) + 1)]
    me_c, me_y, me_d = dev(z, lane_c), dev(z, lane_y), dev(z, lane_d)
    right = lax.rem(ctx + 1, n_ctx)
    left = lax.rem(ctx + n_ctx - 1, n_ctx)

    xs = max(1, n_pipe // 2)
    x, y_hi = pipe // 2, lax.rem(pipe, 2)
    turn = 1 - 2 * core
    y_on = lax.rem(2 * y_hi + y + turn + 4, 4)
    y_back = lax.rem(2 * y_hi + y - turn + 4, 4)

    def across(xx, yy):
        return lax.rem(xx + xs, xs) * 2 + yy // 2, dev(z, 2 * lax.rem(yy, 2) + core)

    relay_to, relay_from = across(x, y_on), across(x, y_back)
    shift_to, shift_from = across(x - (1 - y_back // 2), y_on), across(x + y_hi, y_back)

    def remote(src, dst, snd, rcv, to, where=None):
        return pltpu.make_async_remote_copy(
            src_ref=src, dst_ref=dst, send_sem=snd, recv_sem=rcv,
            device_id=(pipe, to) if where is None else where,
            device_id_type=pl.DeviceIdType.MESH,
        )

    loads = [
        pltpu.make_async_copy(z_ref, z_v, loc_sem.at[0]),
        pltpu.make_async_copy(
            w_ref, w_v.at[pl.ds(pl.multiple_of(ctx * feats, feats), feats)], loc_sem.at[1]
        ),
        pltpu.make_async_copy(q_ref, q_v, loc_sem.at[2]),
        pltpu.make_async_copy(g_ref, g_v, loc_sem.at[3]),
    ]
    for load in loads:
        load.start()

    with jax.named_scope("greet"):
        barrier = pltpu.get_barrier_semaphore()
        greeted = [(pipe, d) for d in (*ups, *downs, me_c, me_y, me_d, right, left)]
        if n_pipe > 1:
            greeted += [relay_to, relay_from, shift_to, shift_from]
        for who in greeted:
            pl.semaphore_signal(barrier, inc=1, device_id=who, device_id_type=pl.DeviceIdType.MESH)
        pl.semaphore_wait(barrier, len(greeted))

    def piece_at(zz, ll):
        return w_v.at[pl.ds(pl.multiple_of((zz * LANES + ll) * feats, feats), feats)]

    def pieces(count):
        return w_v.at[pl.ds(0, count * feats)]

    sent = [0]

    def push(zz, ll, to, came, own=False):
        sent[0] += 1
        remote(w_ref if own else piece_at(zz, ll), piece_at(zz, ll), ag_snd, came, to).start()

    def arrive(count, came):
        remote(pieces(count), pieces(count), ag_snd, came, me_c).wait_recv()

    def shift(hop, part):
        early = 3 * rows // 8
        at = pl.ds(0, early) if part == 0 else pl.ds(early, rows - early)
        if hop == 0:
            return remote(up_ref.at[at], relay.at[at], rl_snd, rl_rcv.at[part], None, relay_to)
        return remote(relay.at[at], up_v.at[at], up_snd, up_rcv, None, shift_to)

    def shift_start(hop, part):
        if n_pipe == 1:
            if (hop, part) == (0, 0):
                pltpu.make_async_copy(up_ref, up_v, up_rcv).start()
            return
        if hop == 1:
            shift(0, part).wait_recv()
        shift(hop, part).start()

    def chain(distance, upward):
        reach, to = (hp, ups) if upward else (hm, downs)
        zz = at_z(-distance if upward else distance)
        for stride in (1, 2, 4) if distance % 4 == 0 else (1,) if distance % 2 == 0 else ():
            if distance + stride <= reach:
                push(zz, lane, to[stride - 1], ag_z.at[int(upward), distance + stride - 1], own=distance == 0)

    chain(0, True)
    chain(0, False)
    push(z, lane, me_y, ag_y.at[0], own=True)
    push(z, lane, me_c, ag_c.at[0], own=True)

    with jax.named_scope("norm"):
        loads[0].wait()
        z_wide = z_v[...].astype(F32)
        factor = lax.rsqrt(jnp.mean(z_wide * z_wide, axis=-1, keepdims=True) + EPSILON)
        fac[...] = jnp.broadcast_to(factor, fac.shape)
        nb[...] = (z_wide * factor).astype(BF16)
        for k in range(zs):
            block = nb[:, k * width:(k + 1) * width].astype(F32)
            nt[k] = block.T.astype(BF16).reshape(LANES, feats, rows)

    def give(ll, to):
        remote(nt.at[:, ll], nt_sh.at[lane], nt_snd, nt_rcv, to).start()
    give(lane_d, me_d)
    give(lane_y, me_y)
    give(lane_c, me_c)
    shift_start(0, 0)
    nt_sh[lane] = nt[:, lane]
    loads[1].wait()
    acc[...] = jnp.zeros_like(acc)

    def project(zz):
        at = pl.multiple_of(zz * width, width)
        acc[...] += dot(nb[:, pl.ds(at, width)], w_v[pl.ds(at, width), :])

    def slices(s):
        if s == 0:
            return [z]
        return ([at_z(-s)] if s <= hp else []) + ([at_z(s)] if s <= hm else [])

    order = [d for d in (1, 2, 4, 3, 5, 6, 8, 7) if d <= hp]
    assert len(order) == hp
    y_lag, c_lag = 4, 6

    def cross(s):
        found = slices(s)
        if s == order[-1]:
            arrive(2 * len(found), ag_y.at[s])
            return
        arrive(len(found), ag_y.at[s])
        for zz in found:
            push(zz, lane_y, me_c, ag_c.at[s])

    order = [0] + order
    for i in range(1, hp + c_lag + 1):
        with jax.named_scope(f"ag{i}"):
            if i <= hp:
                s = order[i]
                for zz, upward in zip(slices(s), (True, False)):
                    arrive(1, ag_z.at[int(upward), s - 1])
                    chain(s, upward)
                    push(zz, lane, me_y, ag_y.at[s])
                    if i == hp:
                        push(zz, lane, me_d, ag_y.at[s])
                    push(zz, lane, me_c, ag_c.at[s])
                for back in range(max(0, i - y_lag), hp + 1) if i == hp else [i - y_lag]:
                    if back >= 0:
                        cross(order[back])
            if i >= c_lag:
                s = order[i - c_lag]
                found = slices(s)
                arrive((1 if s == order[-1] else 2) * len(found), ag_c.at[s])
                for zz in found:
                    project(zz)

    def halo_copies(group):
        own = kvw.at[group, 1]
        return (
            remote(own, kvw.at[group, 0], halo_snd, halo_rcv.at[group], right),
            remote(own, kvw.at[group, 2], halo_snd, halo_rcv.at[group], left),
        )

    for group in range(KV_HEADS):
        at_k, at_v = group * HEAD_DIM, (KV_HEADS + group) * HEAD_DIM
        kvw[group, 1, 0] = acc[:, at_k:at_k + HEAD_DIM].astype(BF16)
        kvw[group, 1, 1] = acc[:, at_v:at_v + HEAD_DIM].astype(BF16)
        for copy in halo_copies(group):
            copy.start()
    loads[2].wait()
    loads[3].wait()

    def halo_wait(group):
        both = kvw.at[group, pl.ds(0, 2)]
        remote(both, both, halo_snd, halo_rcv.at[group], right).wait_recv()

    key_pos = lax.broadcasted_iota(jnp.int32, (rows, rows), 0)
    query_pos = lax.broadcasted_iota(jnp.int32, (rows, rows), 1)
    lower = key_pos >= query_pos
    upper = key_pos <= query_pos

    def attention(group, heads):
        keys = kvw[group, :, 0].reshape(3 * rows, HEAD_DIM)
        values = kvw[group, :, 1].reshape(3 * rows, HEAD_DIM)
        parts = [slice(b * rows, (b + 1) * rows) for b in range(3)]

        def lanes(h):
            return slice((group * PER_GROUP + h) * HEAD_DIM, (group * PER_GROUP + h + 1) * HEAD_DIM)

        def multiply(h):
            slot = h % 2
            scores = dot(keys, q_v[:, lanes(h)], NT)
            s_buf[slot, parts[0]] = jnp.where(lower, scores[parts[0]], -1e30)
            s_buf[slot, parts[1]] = scores[parts[1]]
            s_buf[slot, parts[2]] = jnp.where(upper, scores[parts[2]], -1e30)
            d_buf[slot] = dot(values, g_v[:, lanes(h)], NT)

        def weigh(h):
            slot, into = h % 2, slice(h * HEAD_DIM, (h + 1) * HEAD_DIM)
            peak = jnp.maximum(jnp.maximum(s_buf[slot, parts[0]], s_buf[slot, parts[1]]), s_buf[slot, parts[2]])
            peak = over_keys(jnp.maximum, jnp.max, peak)
            total = row_dot = None
            for part in parts:
                lifted = jnp.exp2((s_buf[slot, part] - peak) * (scale * math.log2(math.e)))
                s_buf[slot, part] = lifted
                product = lifted * d_buf[slot, part]
                total = lifted if total is None else total + lifted
                row_dot = product if row_dot is None else row_dot + product
            inverse = 1.0 / over_keys(jnp.add, jnp.sum, total)
            row_dot = over_keys(jnp.add, jnp.sum, row_dot) * inverse
            for part in parts:
                lifted = s_buf[slot, part]
                p_all[part, into] = (lifted * inverse).astype(BF16)
                d_all[part, into] = (lifted * (inverse * scale) * (d_buf[slot, part] - row_dot)).astype(BF16)

        def spread_query(h):
            into = slice(h * HEAD_DIM, (h + 1) * HEAD_DIM)
            d_query = dot(d_all[:, into], keys, (((0,), (0,)), ((), ())))
            dq_v[:, lanes(h)] = d_query.astype(BF16)

        def sum_heads(first, last):
            into = slice(first * HEAD_DIM, last * HEAD_DIM)
            for ref, source, at in ((d_all, q_v, 0), (p_all, g_v, HEAD_DIM)):
                rest = jnp.concatenate([source[:, lanes(h)] for h in range(first, last)], axis=0)
                total = dot(ref[:, into], rest)
                if first > 0:
                    total = total + dkw[group, :, at:at + HEAD_DIM]
                dkw[group, :, at:at + HEAD_DIM] = total

        half = PER_GROUP // 2
        multiply(heads[0])
        for h in heads:
            if h != heads[-1]:
                multiply(h + 1)
            weigh(h)
            if h != heads[0]:
                spread_query(h - 1)
            if h == half:
                sum_heads(0, half)
        spread_query(heads[-1])
        if heads[-1] == PER_GROUP - 1:
            sum_heads(half, PER_GROUP)

    def fold_start(group):
        for side, start, to in ((0, 2 * rows, right), (1, 0, left)):
            folded[group, side] = dkw[group, start:start + rows].astype(BF16)
            remote(
                folded.at[group, side], fold.at[group, side], fold_snd, fold_rcv.at[group], to
            ).start()

    def share_start(group):
        remote(fold.at[group], fold.at[group], fold_snd, fold_rcv.at[group], right).wait_recv()
        total = dkw[group, rows:2 * rows] + fold[group, 0].astype(F32) + fold[group, 1].astype(F32)
        high = total.astype(BF16)
        low = (total - high.astype(F32)).astype(BF16)
        dkv_sh[lane, group] = high
        at_k, at_v = group * HEAD_DIM, (KV_HEADS + group) * HEAD_DIM
        for into, part in ((dkv_hi, high), (dkv_lo, low)):
            into[:, at_k:at_k + HEAD_DIM] = part[:, :HEAD_DIM]
            into[:, at_v:at_v + HEAD_DIM] = part[:, HEAD_DIM:]
        for kind, to in enumerate((me_y, me_c)):
            share(group, lane, kind, to).start()

    def share(group, ll, kind, to):
        part = dkv_sh.at[ll, group]
        return remote(part, part, sh_snd, sh_rcv.at[group, kind], to)

    def share_pass(group):
        share(group, lane_y, 0, me_c).wait_recv()
        share(group, lane_y, 1, me_c).start()

    def ring_refs(upward):
        if upward:
            return p_snd, p_rcv, p_sent, p_came, ups, hp
        return m_snd, m_rcv, m_sent, m_came, downs, hm

    def ring_send(group, k, upward, total):
        snd, rcv, s_sem, r_sem, to, _ = ring_refs(upward)
        far = int(k > REACH)
        snd[group, k - 1] = total.astype(BF16)
        remote(
            snd.at[group, k - 1], rcv.at[group, k - 1], s_sem, r_sem.at[group, far],
            to[(k - REACH if far else k) - 1],
        ).start()

    def ring_wait(group, upward, first, count, far):
        _, rcv, s_sem, r_sem, to, _ = ring_refs(upward)
        some = rcv.at[group, pl.ds(first, count)]
        remote(some, some, s_sem, r_sem.at[group, far], to[0]).wait_recv()
        return [rcv[group, first + k].astype(F32) for k in range(count)]

    def ring_start(group):
        two = dkv_sh.at[pl.ds(0, 2), group]
        remote(two, two, sh_snd, sh_rcv.at[group, 1], me_c).wait_recv()
        held = jnp.concatenate(
            [nt_sh[p].reshape(zs * feats, rows) for p in range(LANES)], axis=1
        )
        terms = dot(held, dkv_sh[:, group].reshape(LANES * rows, 2 * HEAD_DIM))
        prod[group] = terms.reshape(zs, feats, 2 * HEAD_DIM)
        for k in range(hp, 0, -1):
            for upward, reach in ((True, hp), (False, hm)):
                if k <= reach and (k != REACH or reach <= REACH):
                    ring_send(group, k, upward, prod[group, at_z(k if upward else -k)])

    def ring_middle(group):
        for upward, reach in ((True, hp), (False, hm)):
            if reach > REACH:
                total = prod[group, at_z(REACH if upward else -REACH)]
                for term in ring_wait(group, upward, REACH, reach - REACH, 1):
                    total = total + term
                ring_send(group, REACH, upward, total)

    def ring_end(group):
        total = prod[group, z]
        for upward, reach in ((True, hp), (False, hm)):
            if reach > 0:
                for term in ring_wait(group, upward, 0, min(REACH, reach), 0):
                    total = total + term
        total = total * (1.0 / math.sqrt(rows * n_ctx))
        at_k, at_v = group * HEAD_DIM, (KV_HEADS + group) * HEAD_DIM
        wg_v[:, at_k:at_k + HEAD_DIM] = total[:, :HEAD_DIM]
        wg_v[:, at_v:at_v + HEAD_DIM] = total[:, HEAD_DIM:]

    with jax.named_scope("halo0"):
        halo_wait(0)
    with jax.named_scope("att0"):
        attention(0, range(PER_GROUP))
    fold_start(0)
    with jax.named_scope("halo1"):
        halo_wait(1)
    with jax.named_scope("att1"):
        attention(1, range(PER_GROUP))
    fold_start(1)
    with jax.named_scope("share0"):
        share_start(0)
    with jax.named_scope("nt"):
        three = nt_sh.at[pl.ds(0, LANES - 1)]
        remote(three, three, nt_snd, nt_rcv, me_c).wait_recv()
    with jax.named_scope("pass0"):
        share_pass(0)
    with jax.named_scope("share1"):
        share_start(1)
    shift_start(1, 0)
    shift_start(0, 1)
    with jax.named_scope("ring0"):
        ring_start(0)

    model = z_v.shape[1]
    blocks = 8
    span = model // blocks
    dot_sum[...] = jnp.zeros_like(dot_sum)

    def spread(b):
        w_b = w_v[b * span:(b + 1) * span, :]
        d_b = dot(dkv_hi[...], w_b, NT) + dot(dkv_lo[...], w_b, NT)
        dn[:, b * span:(b + 1) * span] = d_b
        normed = z_v[:, b * span:(b + 1) * span].astype(F32) * fac[:, :1]
        part = d_b * normed
        total = part[:, :128]
        for k in range(1, span // 128):
            total = total + part[:, k * 128:(k + 1) * 128]
        dot_sum[...] += total

    def finish(b, mean):
        at = slice(b * span, (b + 1) * span)
        normed = z_v[:, at].astype(F32) * fac[:, :1]
        branch = fac[:, :1] * (dn[:, at] - normed * mean)
        go_v[:, at] = (up_v[:, at].astype(F32) + branch).astype(BF16)

    todo = [functools.partial(spread, b) for b in range(blocks)]

    def last():
        with jax.named_scope("up"):
            if n_pipe > 1:
                remote(relay, up_v, up_snd, up_rcv, None, shift_to).wait_recv()
            else:
                pltpu.make_async_copy(up_ref, up_v, up_rcv).wait()
        mean = jnp.sum(dot_sum[...], axis=-1, keepdims=True) * (1.0 / model)
        for b in range(blocks):
            finish(b, mean)

    todo.append(last)
    def fill(count):
        for _ in range(count):
            if todo:
                todo.pop(0)()

    def stage(name, act):
        with jax.named_scope(name):
            act()

    stage("fill0", lambda: fill(3))
    stage("pass1", lambda: share_pass(1))
    stage("fill1", lambda: fill(1))
    stage("ring1", lambda: ring_start(1))
    stage("fill1", lambda: fill(2))
    stage("mid0", lambda: ring_middle(0))
    stage("fwd", lambda: shift_start(1, 1))
    stage("fill2", lambda: fill(2))
    stage("mid1", lambda: ring_middle(1))
    stage("end0", lambda: ring_end(0))
    stage("last", lambda: fill(len(todo)))
    stage("end1", lambda: ring_end(1))

    with jax.named_scope("drain"):
        all_sent = [
            (pieces(sent[0]), ag_snd), (nt.at[:, pl.ds(0, LANES - 1)], nt_snd),
            (kvw.at[:, pl.ds(0, 2)], halo_snd), (fold, fold_snd),
            (dkv_sh.at[pl.ds(0, LANES - 1)], sh_snd), (p_snd, p_sent),
        ]
        if hm > 0:
            all_sent.append((m_snd, m_sent))
        if n_pipe > 1:
            all_sent += [(up_v, up_snd), (relay, rl_snd)]
        for ref, sem in all_sent:
            remote(ref, ref, sem, sem, me_c).wait_send()


def store(go_v, dq_v, wg_v, go_ref, dq_ref, wg_ref, sem):
    copies = [
        pltpu.make_async_copy(src, dst, sem.at[i])
        for i, (src, dst) in enumerate(((go_v, go_ref), (dq_v, dq_ref), (wg_v, wg_ref)))
    ]
    for copy in copies:
        copy.start()
    for copy in copies:
        copy.wait()


def per_device(n_pipe, n_ctx, saved_in, grad_in, queries, d_heads, kv_weights):
    rows, model = saved_in.shape[1:]
    feats, kv_all = kv_weights.shape[1:]
    zs = n_ctx // LANES
    hp = zs // 2
    hm = max(1, zs - 1 - hp)
    pair = 2 * HEAD_DIM
    vm = pltpu.VMEM
    dma = pltpu.SemaphoreType.DMA
    big = vm((rows, model), BF16)
    scratch = [
        big, big, big, big, big,
        big, vm((rows, 128), F32),
        vm((zs, LANES, feats, rows), BF16), vm((LANES, zs, feats, rows), BF16),
        vm((n_ctx * feats, kv_all), BF16), vm((KV_HEADS, 3, 2, rows, HEAD_DIM), BF16), vm((rows, kv_all), F32),
        vm((KV_HEADS, 3 * rows, pair), F32), vm((KV_HEADS, 2, rows, pair), BF16), vm((KV_HEADS, 2, rows, pair), BF16),
        vm((rows, kv_all), BF16), vm((rows, kv_all), BF16),
        vm((LANES, KV_HEADS, rows, pair), BF16), vm((KV_HEADS, zs, feats, pair), F32),
        vm((rows, model), F32), vm((rows, 128), F32),
        vm((KV_HEADS, hp, feats, pair), BF16), vm((KV_HEADS, hp, feats, pair), BF16),
        vm((KV_HEADS, hm, feats, pair), BF16), vm((KV_HEADS, hm, feats, pair), BF16),
        vm((2, 3 * rows, HEAD_DIM), F32), vm((2, 3 * rows, HEAD_DIM), F32),
        vm((3 * rows, PER_GROUP * HEAD_DIM), BF16), vm((3 * rows, PER_GROUP * HEAD_DIM), BF16),
        dma((4,)), dma, dma((2, hp)), dma((hp + 1,)), dma((hp + 1,)),
        dma, dma, dma, dma, dma, dma((2,)),
        dma, dma((KV_HEADS,)), dma, dma((KV_HEADS,)),
        dma, dma((KV_HEADS, 2)),
        dma, dma((KV_HEADS, 2)), dma, dma((KV_HEADS, 2)),
    ]
    hbm = pl.BlockSpec(memory_space=pltpu.HBM)
    vmem = pl.BlockSpec(memory_space=pltpu.VMEM)
    shapes = (
        jax.ShapeDtypeStruct((rows, model), BF16),
        jax.ShapeDtypeStruct((rows, model), BF16),
        jax.ShapeDtypeStruct((feats, kv_all), F32),
    )
    results = pl.pallas_call(
        functools.partial(kernel, n_pipe, n_ctx),
        out_shape=shapes,
        in_specs=[hbm] * 5,
        out_specs=(vmem,) * 3,
        scratch_shapes=scratch,
        compiler_params=pltpu.CompilerParams(
            collective_id=0, has_side_effects=True, vmem_limit_bytes=48 * 1024 * 1024
        ),
        name="step",
    )(*(
        pltpu.with_memory_space_constraint(x[0], pltpu.HBM)
        for x in (saved_in, grad_in, queries, d_heads, kv_weights)
    ))
    grad_out, d_queries, weight_grad = pl.pallas_call(
        store,
        out_shape=shapes,
        in_specs=[vmem] * 3,
        out_specs=(hbm,) * 3,
        scratch_shapes=[dma((3,))],
        name="store",
    )(*(pltpu.with_memory_space_constraint(x, pltpu.VMEM) for x in results))
    return grad_out[None], d_queries[None], weight_grad[None]


def solution(mesh):
    spec = P("pipe", "ctx", None)
    return jax.shard_map(
        functools.partial(per_device, mesh.shape["pipe"], mesh.shape["ctx"]),
        mesh=mesh, in_specs=(spec,) * 5, out_specs=(spec,) * 3, check_vma=False,
    )
```

```python
import functools
import math

import jax
import jax.numpy as jnp
from jax import lax
from jax.experimental import pallas as pl
from jax.experimental.pallas import tpu as pltpu
from jax.sharding import PartitionSpec as P

HEADS = 16
HEAD_DIM = 128
KV_HEADS = 2
PER_GROUP = HEADS // KV_HEADS
LANES = 4
REACH = 4
EPSILON = 1e-06

F32 = jnp.float32
BF16 = jnp.bfloat16
NT = (((1,), (1,)), ((), ()))


def dot(a, b, dims=(((1,), (0,)), ((), ()))):
    return lax.dot_general(a, b, dims, preferred_element_type=F32)


def over_keys(op, last, a):
    while a.shape[0] > 8:
        parts = 3 if a.shape[0] % 3 == 0 else 2
        step = a.shape[0] // parts
        total = a[:step]
        for k in range(1, parts):
            total = op(total, a[k * step:(k + 1) * step])
        a = total
    return last(a, axis=0, keepdims=True)


def kernel(
    n_pipe, n_ctx,
    z_ref, up_ref, q_ref, g_ref, w_ref,
    go_v, dq_v, wg_v,
    z_v, q_v, g_v, up_v, relay,
    nb, fac, nt, nt_sh, w_v, kvw, acc,
    dkw, folded, fold, dkv_hi, dkv_lo, dkv_sh, prod, dn, dot_sum,
    p_snd, p_rcv, m_snd, m_rcv,
    s_buf, d_buf, p_all, d_all,
    loc_sem, ag_snd, ag_z, ag_y, ag_c,
    nt_snd, nt_rcv, up_snd, up_rcv, rl_snd, rl_rcv,
    halo_snd, halo_rcv, fold_snd, fold_rcv,
    sh_snd, sh_rcv,
    p_sent, p_came, m_sent, m_came,
):
    rows = z_v.shape[0]
    zs = n_ctx // LANES
    hp = zs // 2
    hm = zs - 1 - hp
    feats = w_ref.shape[0]
    width = LANES * feats
    scale = 1.0 / math.sqrt(HEAD_DIM)

    pipe = lax.axis_index("pipe")
    ctx = lax.axis_index("ctx")
    z = ctx // LANES
    lane = lax.rem(ctx, LANES)
    y = lane // 2
    core = lax.rem(lane, 2)
    lane_c = 2 * y + (1 - core)
    lane_y = 2 * (1 - y) + core
    lane_d = 2 * (1 - y) + (1 - core)

    def at_z(distance):
        return lax.rem(z + distance + zs, zs)

    def dev(zz, ll):
        return zz * LANES + ll

    ups = [dev(at_z(k), lane) for k in range(1, min(max(4, REACH), hp) + 1)]
    downs = [dev(at_z(-k), lane) for k in range(1, min(max(4, REACH), hp) + 1)]
    me_c, me_y, me_d = dev(z, lane_c), dev(z, lane_y), dev(z, lane_d)
    right = lax.rem(ctx + 1, n_ctx)
    left = lax.rem(ctx + n_ctx - 1, n_ctx)

    xs = max(1, n_pipe // 2)
    x, y_hi = pipe // 2, lax.rem(pipe, 2)
    turn = 1 - 2 * core
    y_on = lax.rem(2 * y_hi + y + turn + 4, 4)
    y_back = lax.rem(2 * y_hi + y - turn + 4, 4)

    def across(xx, yy):
        return lax.rem(xx + xs, xs) * 2 + yy // 2, dev(z, 2 * lax.rem(yy, 2) + core)

    relay_to, relay_from = across(x, y_on), across(x, y_back)
    shift_to, shift_from = across(x - (1 - y_back // 2), y_on), across(x + y_hi, y_back)

    def remote(src, dst, snd, rcv, to, where=None):
        return pltpu.make_async_remote_copy(
            src_ref=src, dst_ref=dst, send_sem=snd, recv_sem=rcv,
            device_id=(pipe, to) if where is None else where,
            device_id_type=pl.DeviceIdType.MESH,
        )

    loads = [
        pltpu.make_async_copy(z_ref, z_v, loc_sem.at[0]),
        pltpu.make_async_copy(
            w_ref, w_v.at[pl.ds(pl.multiple_of(ctx * feats, feats), feats)], loc_sem.at[1]
        ),
        pltpu.make_async_copy(q_ref, q_v, loc_sem.at[2]),
        pltpu.make_async_copy(g_ref, g_v, loc_sem.at[3]),
    ]
    for load in loads:
        load.start()

    with jax.named_scope("greet"):
        barrier = pltpu.get_barrier_semaphore()
        greeted = [(pipe, d) for d in (*ups, *downs, me_c, me_y, me_d, right, left)]
        if n_pipe > 1:
            greeted += [relay_to, relay_from, shift_to, shift_from]
        for who in greeted:
            pl.semaphore_signal(barrier, inc=1, device_id=who, device_id_type=pl.DeviceIdType.MESH)
        pl.semaphore_wait(barrier, len(greeted))

    def piece_at(zz, ll):
        return w_v.at[pl.ds(pl.multiple_of((zz * LANES + ll) * feats, feats), feats)]

    def pieces(count):
        return w_v.at[pl.ds(0, count * feats)]

    sent = [0]

    def push(zz, ll, to, came, own=False):
        sent[0] += 1
        remote(w_ref if own else piece_at(zz, ll), piece_at(zz, ll), ag_snd, came, to).start()

    def arrive(count, came):
        remote(pieces(count), pieces(count), ag_snd, came, me_c).wait_recv()

    def shift(hop, part):
        early = 3 * rows // 8
        at = pl.ds(0, early) if part == 0 else pl.ds(early, rows - early)
        if hop == 0:
            return remote(up_ref.at[at], relay.at[at], rl_snd, rl_rcv.at[part], None, relay_to)
        return remote(relay.at[at], up_v.at[at], up_snd, up_rcv, None, shift_to)

    def shift_start(hop, part):
        if n_pipe == 1:
            if (hop, part) == (0, 0):
                pltpu.make_async_copy(up_ref, up_v, up_rcv).start()
            return
        if hop == 1:
            shift(0, part).wait_recv()
        shift(hop, part).start()

    def chain(distance, upward):
        reach, to = (hp, ups) if upward else (hm, downs)
        zz = at_z(-distance if upward else distance)
        strides = {0: (1, 2, 4), 2: (1,), 4: (1, 2, 3, 4)}
        for stride in strides.get(distance, ()):
            if distance + stride <= reach:
                push(zz, lane, to[stride - 1], ag_z.at[int(upward), distance + stride - 1], own=distance == 0)

    chain(0, True)
    chain(0, False)
    push(z, lane, me_y, ag_y.at[0], own=True)
    push(z, lane, me_c, ag_c.at[0], own=True)

    with jax.named_scope("norm"):
        loads[0].wait()
        z_wide = z_v[...].astype(F32)
        factor = lax.rsqrt(jnp.mean(z_wide * z_wide, axis=-1, keepdims=True) + EPSILON)
        fac[...] = jnp.broadcast_to(factor, fac.shape)
        nb[...] = (z_wide * factor).astype(BF16)
        for k in range(zs):
            block = nb[:, k * width:(k + 1) * width].astype(F32)
            nt[k] = block.T.astype(BF16).reshape(LANES, feats, rows)

    def give(ll, to):
        remote(nt.at[:, ll], nt_sh.at[lane], nt_snd, nt_rcv, to).start()
    give(lane_d, me_d)
    give(lane_c, me_c)
    nt_sh[lane] = nt[:, lane]
    loads[1].wait()
    acc[...] = jnp.zeros_like(acc)

    def project(zz):
        at = pl.multiple_of(zz * width, width)
        acc[...] += dot(nb[:, pl.ds(at, width)], w_v[pl.ds(at, width), :])

    def slices(s):
        if s == 0:
            return [z]
        return ([at_z(-s)] if s <= hp else []) + ([at_z(s)] if s <= hm else [])

    order = [d for d in (1, 2, 4, 3, 5, 6, 7, 8) if d <= hp]
    assert len(order) == hp
    y_lag, c_lag = 7, 8

    def cross(s):
        found = slices(s)
        if s == order[-1]:
            arrive(2 * len(found), ag_y.at[s])
            return
        arrive(len(found), ag_y.at[s])
        for zz in found:
            push(zz, lane_y, me_c, ag_c.at[s])

    order = [0] + order
    for i in range(1, hp + c_lag + 1):
        with jax.named_scope(f"ag{i}"):
            if i <= hp:
                s = order[i]
                for zz, upward in zip(slices(s), (True, False)):
                    arrive(1, ag_z.at[int(upward), s - 1])
                    chain(s, upward)
                    push(zz, lane, me_y, ag_y.at[s])
                    if i == hp:
                        push(zz, lane, me_d, ag_y.at[s])
                    push(zz, lane, me_c, ag_c.at[s])
                if i == hp:
                    give(lane_y, me_y)
                    shift_start(0, 0)
                for back in range(max(0, i - y_lag), hp + 1) if i == hp else [i - y_lag]:
                    if back >= 0:
                        cross(order[back])
            if i >= c_lag:
                s = order[i - c_lag]
                found = slices(s)
                arrive((1 if s == order[-1] else 2) * len(found), ag_c.at[s])
                for zz in found:
                    project(zz)

    def halo_copies(group):
        own = kvw.at[group, 1]
        return (
            remote(own, kvw.at[group, 0], halo_snd, halo_rcv.at[group], right),
            remote(own, kvw.at[group, 2], halo_snd, halo_rcv.at[group], left),
        )

    for group in range(KV_HEADS):
        at_k, at_v = group * HEAD_DIM, (KV_HEADS + group) * HEAD_DIM
        kvw[group, 1, 0] = acc[:, at_k:at_k + HEAD_DIM].astype(BF16)
        kvw[group, 1, 1] = acc[:, at_v:at_v + HEAD_DIM].astype(BF16)
        for copy in halo_copies(group):
            copy.start()
    loads[2].wait()
    loads[3].wait()

    def halo_wait(group):
        both = kvw.at[group, pl.ds(0, 2)]
        remote(both, both, halo_snd, halo_rcv.at[group], right).wait_recv()

    key_pos = lax.broadcasted_iota(jnp.int32, (rows, rows), 0)
    query_pos = lax.broadcasted_iota(jnp.int32, (rows, rows), 1)
    lower = key_pos >= query_pos
    upper = key_pos <= query_pos

    def attention(group, heads):
        keys = kvw[group, :, 0].reshape(3 * rows, HEAD_DIM)
        values = kvw[group, :, 1].reshape(3 * rows, HEAD_DIM)
        parts = [slice(b * rows, (b + 1) * rows) for b in range(3)]

        def lanes(h):
            return slice((group * PER_GROUP + h) * HEAD_DIM, (group * PER_GROUP + h + 1) * HEAD_DIM)

        def multiply(h):
            slot = h % 2
            scores = dot(keys, q_v[:, lanes(h)], NT)
            s_buf[slot, parts[0]] = jnp.where(lower, scores[parts[0]], -1e30)
            s_buf[slot, parts[1]] = scores[parts[1]]
            s_buf[slot, parts[2]] = jnp.where(upper, scores[parts[2]], -1e30)
            d_buf[slot] = dot(values, g_v[:, lanes(h)], NT)

        def weigh(h):
            slot, into = h % 2, slice(h * HEAD_DIM, (h + 1) * HEAD_DIM)
            peak = jnp.maximum(jnp.maximum(s_buf[slot, parts[0]], s_buf[slot, parts[1]]), s_buf[slot, parts[2]])
            peak = over_keys(jnp.maximum, jnp.max, peak)
            total = row_dot = None
            for part in parts:
                lifted = jnp.exp2((s_buf[slot, part] - peak) * (scale * math.log2(math.e)))
                s_buf[slot, part] = lifted
                product = lifted * d_buf[slot, part]
                total = lifted if total is None else total + lifted
                row_dot = product if row_dot is None else row_dot + product
            inverse = 1.0 / over_keys(jnp.add, jnp.sum, total)
            row_dot = over_keys(jnp.add, jnp.sum, row_dot) * inverse
            for part in parts:
                lifted = s_buf[slot, part]
                p_all[part, into] = (lifted * inverse).astype(BF16)
                d_all[part, into] = (lifted * (inverse * scale) * (d_buf[slot, part] - row_dot)).astype(BF16)

        def spread_query(h):
            into = slice(h * HEAD_DIM, (h + 1) * HEAD_DIM)
            d_query = dot(d_all[:, into], keys, (((0,), (0,)), ((), ())))
            dq_v[:, lanes(h)] = d_query.astype(BF16)

        def sum_heads(first, last):
            into = slice(first * HEAD_DIM, last * HEAD_DIM)
            for ref, source, at in ((d_all, q_v, 0), (p_all, g_v, HEAD_DIM)):
                rest = jnp.concatenate([source[:, lanes(h)] for h in range(first, last)], axis=0)
                total = dot(ref[:, into], rest)
                if first > 0:
                    total = total + dkw[group, :, at:at + HEAD_DIM]
                dkw[group, :, at:at + HEAD_DIM] = total

        half = PER_GROUP // 2
        multiply(heads[0])
        for h in heads:
            if h != heads[-1]:
                multiply(h + 1)
            weigh(h)
            if h != heads[0]:
                spread_query(h - 1)
            if h == half:
                sum_heads(0, half)
        spread_query(heads[-1])
        if heads[-1] == PER_GROUP - 1:
            sum_heads(half, PER_GROUP)

    def fold_start(group):
        for side, start, to in ((0, 2 * rows, right), (1, 0, left)):
            folded[group, side] = dkw[group, start:start + rows].astype(BF16)
            remote(
                folded.at[group, side], fold.at[group, side], fold_snd, fold_rcv.at[group], to
            ).start()

    def share_start(group):
        remote(fold.at[group], fold.at[group], fold_snd, fold_rcv.at[group], right).wait_recv()
        total = dkw[group, rows:2 * rows] + fold[group, 0].astype(F32) + fold[group, 1].astype(F32)
        high = total.astype(BF16)
        low = (total - high.astype(F32)).astype(BF16)
        dkv_sh[lane, group] = high
        at_k, at_v = group * HEAD_DIM, (KV_HEADS + group) * HEAD_DIM
        for into, part in ((dkv_hi, high), (dkv_lo, low)):
            into[:, at_k:at_k + HEAD_DIM] = part[:, :HEAD_DIM]
            into[:, at_v:at_v + HEAD_DIM] = part[:, HEAD_DIM:]
        for kind, to in enumerate((me_y, me_c)):
            share(group, lane, kind, to).start()

    def share(group, ll, kind, to):
        part = dkv_sh.at[ll, group]
        return remote(part, part, sh_snd, sh_rcv.at[group, kind], to)

    def share_pass(group):
        share(group, lane_y, 0, me_c).wait_recv()
        share(group, lane_y, 1, me_c).start()

    def ring_refs(upward):
        if upward:
            return p_snd, p_rcv, p_sent, p_came, ups, hp
        return m_snd, m_rcv, m_sent, m_came, downs, hm

    def relayed(k):
        return k == 3 and REACH > 3

    def ring_slot(k):
        return {3: 3, 4: 2}.get(k, k - 1) if REACH > 3 else k - 1

    def ring_send(group, k, upward, total):
        snd, rcv, s_sem, r_sem, to, reach = ring_refs(upward)
        slot = k - 1 if reach < 4 else ring_slot(k)
        kind, step = (2, 1) if relayed(k) else (1, k - REACH) if k > REACH else (0, k)
        snd[group, slot] = total.astype(BF16)
        remote(
            snd.at[group, slot], rcv.at[group, slot], s_sem, r_sem.at[group, kind], to[step - 1]
        ).start()

    def ring_wait(group, upward, first, count, kind):
        _, rcv, s_sem, r_sem, to, _ = ring_refs(upward)
        some = rcv.at[group, pl.ds(first, count)]
        remote(some, some, s_sem, r_sem.at[group, kind], to[0]).wait_recv()
        return [rcv[group, first + k].astype(F32) for k in range(count)]

    def ring_start(group):
        two = dkv_sh.at[pl.ds(0, 2), group]
        remote(two, two, sh_snd, sh_rcv.at[group, 1], me_c).wait_recv()
        held = jnp.concatenate(
            [nt_sh[p].reshape(zs * feats, rows) for p in range(LANES)], axis=1
        )
        terms = dot(held, dkv_sh[:, group].reshape(LANES * rows, 2 * HEAD_DIM))
        prod[group] = terms.reshape(zs, feats, 2 * HEAD_DIM)
        for k in range(hp, REACH, -1):
            ring_both(group, k)

    def ring_both(group, k):
        for upward, reach in ((True, hp), (False, hm)):
            if k <= reach and (k != REACH or reach <= REACH):
                ring_send(group, k, upward, prod[group, at_z(k if upward else -k)])

    def ring_near(group):
        for k in range(min(REACH, hp), 0, -1):
            if k != 2:
                ring_both(group, k)

    def ring_next(group):
        for upward, reach in ((True, hp), (False, hm)):
            if reach >= 2 and REACH >= 2:
                total = prod[group, at_z(2 if upward else -2)]
                if reach >= 3 and REACH > 3:
                    (term,) = ring_wait(group, upward, 2 if reach < 4 else 3, 1, 2)
                    total = total + term
                ring_send(group, 2, upward, total)

    def ring_middle(group):
        for upward, reach in ((True, hp), (False, hm)):
            if reach > REACH:
                total = prod[group, at_z(REACH if upward else -REACH)]
                for term in ring_wait(group, upward, REACH, reach - REACH, 1):
                    total = total + term
                ring_send(group, REACH, upward, total)

    def ring_end(group):
        total = prod[group, z]
        for upward, reach in ((True, hp), (False, hm)):
            if reach > 0:
                near = min(REACH, reach)
                for term in ring_wait(group, upward, 0, near - int(near >= 3 and REACH > 3), 0):
                    total = total + term
        total = total * (1.0 / math.sqrt(rows * n_ctx))
        at_k, at_v = group * HEAD_DIM, (KV_HEADS + group) * HEAD_DIM
        wg_v[:, at_k:at_k + HEAD_DIM] = total[:, :HEAD_DIM]
        wg_v[:, at_v:at_v + HEAD_DIM] = total[:, HEAD_DIM:]

    with jax.named_scope("halo0"):
        halo_wait(0)
    with jax.named_scope("att0"):
        attention(0, range(PER_GROUP))
    fold_start(0)
    with jax.named_scope("halo1"):
        halo_wait(1)
    with jax.named_scope("att1"):
        attention(1, range(PER_GROUP))
    fold_start(1)
    with jax.named_scope("share0"):
        share_start(0)
    with jax.named_scope("nt"):
        three = nt_sh.at[pl.ds(0, LANES - 1)]
        remote(three, three, nt_snd, nt_rcv, me_c).wait_recv()
    with jax.named_scope("share1"):
        share_start(1)
    with jax.named_scope("pass0"):
        share_pass(0)
    shift_start(1, 0)
    shift_start(0, 1)
    with jax.named_scope("ring0"):
        ring_start(0)

    model = z_v.shape[1]
    blocks = 8
    span = model // blocks
    dot_sum[...] = jnp.zeros_like(dot_sum)

    def spread(b):
        w_b = w_v[b * span:(b + 1) * span, :]
        d_b = dot(dkv_hi[...], w_b, NT) + dot(dkv_lo[...], w_b, NT)
        dn[:, b * span:(b + 1) * span] = d_b
        normed = z_v[:, b * span:(b + 1) * span].astype(F32) * fac[:, :1]
        part = d_b * normed
        total = part[:, :128]
        for k in range(1, span // 128):
            total = total + part[:, k * 128:(k + 1) * 128]
        dot_sum[...] += total

    def finish(b, mean):
        at = slice(b * span, (b + 1) * span)
        normed = z_v[:, at].astype(F32) * fac[:, :1]
        branch = fac[:, :1] * (dn[:, at] - normed * mean)
        go_v[:, at] = (up_v[:, at].astype(F32) + branch).astype(BF16)

    todo = [functools.partial(spread, b) for b in range(blocks)]

    def last():
        with jax.named_scope("up"):
            if n_pipe > 1:
                remote(relay, up_v, up_snd, up_rcv, None, shift_to).wait_recv()
            else:
                pltpu.make_async_copy(up_ref, up_v, up_rcv).wait()
        mean = jnp.sum(dot_sum[...], axis=-1, keepdims=True) * (1.0 / model)
        for b in range(blocks):
            finish(b, mean)

    todo.append(last)
    def fill(count):
        for _ in range(count):
            if todo:
                todo.pop(0)()

    def stage(name, act):
        with jax.named_scope(name):
            act()

    stage("fill0", lambda: fill(3))
    stage("pass1", lambda: share_pass(1))
    stage("fill1", lambda: fill(1))
    stage("ring1", lambda: ring_start(1))
    stage("fill1", lambda: fill(2))
    stage("near", lambda: (ring_near(0), ring_near(1)))
    stage("mid0", lambda: ring_middle(0))
    stage("fwd", lambda: shift_start(1, 1))
    stage("fill2", lambda: fill(2))
    stage("mid1", lambda: ring_middle(1))
    stage("next", lambda: (ring_next(0), ring_next(1)))
    stage("end0", lambda: ring_end(0))
    stage("last", lambda: fill(len(todo)))
    stage("end1", lambda: ring_end(1))

    with jax.named_scope("drain"):
        all_sent = [
            (pieces(sent[0]), ag_snd), (nt.at[:, pl.ds(0, LANES - 1)], nt_snd),
            (kvw.at[:, pl.ds(0, 2)], halo_snd), (fold, fold_snd),
            (dkv_sh.at[pl.ds(0, LANES - 1)], sh_snd), (p_snd, p_sent),
        ]
        if hm > 0:
            all_sent.append((m_snd, m_sent))
        if n_pipe > 1:
            all_sent += [(up_v, up_snd), (relay, rl_snd)]
        for ref, sem in all_sent:
            remote(ref, ref, sem, sem, me_c).wait_send()


def store(go_v, dq_v, wg_v, go_ref, dq_ref, wg_ref, sem):
    copies = [
        pltpu.make_async_copy(src, dst, sem.at[i])
        for i, (src, dst) in enumerate(((go_v, go_ref), (dq_v, dq_ref), (wg_v, wg_ref)))
    ]
    for copy in copies:
        copy.start()
    for copy in copies:
        copy.wait()


def per_device(n_pipe, n_ctx, saved_in, grad_in, queries, d_heads, kv_weights):
    rows, model = saved_in.shape[1:]
    feats, kv_all = kv_weights.shape[1:]
    zs = n_ctx // LANES
    hp = zs // 2
    hm = max(1, zs - 1 - hp)
    pair = 2 * HEAD_DIM
    vm = pltpu.VMEM
    dma = pltpu.SemaphoreType.DMA
    big = vm((rows, model), BF16)
    scratch = [
        big, big, big, big, big,
        big, vm((rows, 128), F32),
        vm((zs, LANES, feats, rows), BF16), vm((LANES, zs, feats, rows), BF16),
        vm((n_ctx * feats, kv_all), BF16), vm((KV_HEADS, 3, 2, rows, HEAD_DIM), BF16), vm((rows, kv_all), F32),
        vm((KV_HEADS, 3 * rows, pair), F32), vm((KV_HEADS, 2, rows, pair), BF16), vm((KV_HEADS, 2, rows, pair), BF16),
        vm((rows, kv_all), BF16), vm((rows, kv_all), BF16),
        vm((LANES, KV_HEADS, rows, pair), BF16), vm((KV_HEADS, zs, feats, pair), F32),
        vm((rows, model), F32), vm((rows, 128), F32),
        vm((KV_HEADS, hp, feats, pair), BF16), vm((KV_HEADS, hp, feats, pair), BF16),
        vm((KV_HEADS, hm, feats, pair), BF16), vm((KV_HEADS, hm, feats, pair), BF16),
        vm((2, 3 * rows, HEAD_DIM), F32), vm((2, 3 * rows, HEAD_DIM), F32),
        vm((3 * rows, PER_GROUP * HEAD_DIM), BF16), vm((3 * rows, PER_GROUP * HEAD_DIM), BF16),
        dma((4,)), dma, dma((2, hp)), dma((hp + 1,)), dma((hp + 1,)),
        dma, dma, dma, dma, dma, dma((2,)),
        dma, dma((KV_HEADS,)), dma, dma((KV_HEADS,)),
        dma, dma((KV_HEADS, 2)),
        dma, dma((KV_HEADS, 3)), dma, dma((KV_HEADS, 3)),
    ]
    hbm = pl.BlockSpec(memory_space=pltpu.HBM)
    vmem = pl.BlockSpec(memory_space=pltpu.VMEM)
    shapes = (
        jax.ShapeDtypeStruct((rows, model), BF16),
        jax.ShapeDtypeStruct((rows, model), BF16),
        jax.ShapeDtypeStruct((feats, kv_all), F32),
    )
    results = pl.pallas_call(
        functools.partial(kernel, n_pipe, n_ctx),
        out_shape=shapes,
        in_specs=[hbm] * 5,
        out_specs=(vmem,) * 3,
        scratch_shapes=scratch,
        compiler_params=pltpu.CompilerParams(
            collective_id=0, has_side_effects=True, vmem_limit_bytes=48 * 1024 * 1024
        ),
        name="step",
    )(*(
        pltpu.with_memory_space_constraint(x[0], pltpu.HBM)
        for x in (saved_in, grad_in, queries, d_heads, kv_weights)
    ))
    grad_out, d_queries, weight_grad = pl.pallas_call(
        store,
        out_shape=shapes,
        in_specs=[vmem] * 3,
        out_specs=(hbm,) * 3,
        scratch_shapes=[dma((3,))],
        name="store",
    )(*(pltpu.with_memory_space_constraint(x, pltpu.VMEM) for x in results))
    return grad_out[None], d_queries[None], weight_grad[None]


def solution(mesh):
    spec = P("pipe", "ctx", None)
    return jax.shard_map(
        functools.partial(per_device, mesh.shape["pipe"], mesh.shape["ctx"]),
        mesh=mesh, in_specs=(spec,) * 5, out_specs=(spec,) * 3, check_vma=False,
    )
```

```python
import functools
import math

import jax
import jax.numpy as jnp
from jax import lax
from jax.experimental import pallas as pl
from jax.experimental.pallas import tpu as pltpu
from jax.sharding import PartitionSpec as P

HEADS = 16
HEAD_DIM = 128
KV_HEADS = 2
PER_GROUP = HEADS // KV_HEADS
LANES = 4
REACH = 4
EPSILON = 1e-06

F32 = jnp.float32
BF16 = jnp.bfloat16
NT = (((1,), (1,)), ((), ()))


def dot(a, b, dims=(((1,), (0,)), ((), ()))):
    return lax.dot_general(a, b, dims, preferred_element_type=F32)


def over_keys(op, last, a):
    while a.shape[0] > 8:
        parts = 3 if a.shape[0] % 3 == 0 else 2
        step = a.shape[0] // parts
        total = a[:step]
        for k in range(1, parts):
            total = op(total, a[k * step:(k + 1) * step])
        a = total
    return last(a, axis=0, keepdims=True)


def kernel(
    n_pipe, n_ctx,
    z_ref, up_ref, q_ref, g_ref, w_ref,
    go_v, dq_v, wg_v,
    z_v, q_v, g_v, up_v, relay,
    nb, fac, nt, nt_sh, w_v, kvw, acc,
    dkw, folded, fold, dkv_hi, dkv_lo, dkv_sh, prod, dn, dot_sum,
    p_snd, p_rcv, m_snd, m_rcv,
    s_buf, d_buf, p_all, d_all,
    loc_sem, ag_snd, ag_z, ag_y, ag_c,
    nt_snd, nt_rcv, up_snd, up_rcv, rl_snd, rl_rcv,
    halo_snd, halo_rcv, fold_snd, fold_rcv,
    sh_snd, sh_rcv,
    p_sent, p_came, m_sent, m_came,
):
    rows = z_v.shape[0]
    zs = n_ctx // LANES
    hp = zs // 2
    hm = zs - 1 - hp
    feats = w_ref.shape[0]
    width = LANES * feats
    scale = 1.0 / math.sqrt(HEAD_DIM)

    pipe = lax.axis_index("pipe")
    ctx = lax.axis_index("ctx")
    z = ctx // LANES
    lane = lax.rem(ctx, LANES)
    y = lane // 2
    core = lax.rem(lane, 2)
    lane_c = 2 * y + (1 - core)
    lane_y = 2 * (1 - y) + core
    lane_d = 2 * (1 - y) + (1 - core)

    def at_z(distance):
        return lax.rem(z + distance + zs, zs)

    def dev(zz, ll):
        return zz * LANES + ll

    ups = [dev(at_z(k), lane) for k in range(1, min(max(4, REACH), hp) + 1)]
    downs = [dev(at_z(-k), lane) for k in range(1, min(max(4, REACH), hp) + 1)]
    me_c, me_y, me_d = dev(z, lane_c), dev(z, lane_y), dev(z, lane_d)
    right = lax.rem(ctx + 1, n_ctx)
    left = lax.rem(ctx + n_ctx - 1, n_ctx)

    xs = max(1, n_pipe // 2)
    x, y_hi = pipe // 2, lax.rem(pipe, 2)
    turn = 1 - 2 * core
    y_on = lax.rem(2 * y_hi + y + turn + 4, 4)
    y_back = lax.rem(2 * y_hi + y - turn + 4, 4)

    def across(xx, yy):
        return lax.rem(xx + xs, xs) * 2 + yy // 2, dev(z, 2 * lax.rem(yy, 2) + core)

    relay_to, relay_from = across(x, y_on), across(x, y_back)
    shift_to, shift_from = across(x - (1 - y_back // 2), y_on), across(x + y_hi, y_back)

    def remote(src, dst, snd, rcv, to, where=None):
        return pltpu.make_async_remote_copy(
            src_ref=src, dst_ref=dst, send_sem=snd, recv_sem=rcv,
            device_id=(pipe, to) if where is None else where,
            device_id_type=pl.DeviceIdType.MESH,
        )

    loads = [
        pltpu.make_async_copy(z_ref, z_v, loc_sem.at[0]),
        pltpu.make_async_copy(
            w_ref, w_v.at[pl.ds(pl.multiple_of(ctx * feats, feats), feats)], loc_sem.at[1]
        ),
        pltpu.make_async_copy(q_ref, q_v, loc_sem.at[2]),
        pltpu.make_async_copy(g_ref, g_v, loc_sem.at[3]),
    ]
    for load in loads:
        load.start()

    with jax.named_scope("greet"):
        barrier = pltpu.get_barrier_semaphore()
        greeted = [(pipe, d) for d in (*ups, *downs, me_c, me_y, me_d, right, left)]
        if n_pipe > 1:
            greeted += [relay_to, relay_from, shift_to, shift_from]
        for who in greeted:
            pl.semaphore_signal(barrier, inc=1, device_id=who, device_id_type=pl.DeviceIdType.MESH)
        pl.semaphore_wait(barrier, len(greeted))

    def piece_at(zz, ll):
        return w_v.at[pl.ds(pl.multiple_of((zz * LANES + ll) * feats, feats), feats)]

    def pieces(count):
        return w_v.at[pl.ds(0, count * feats)]

    sent = [0]

    def push(zz, ll, to, came, own=False):
        sent[0] += 1
        remote(w_ref if own else piece_at(zz, ll), piece_at(zz, ll), ag_snd, came, to).start()

    def arrive(count, came):
        remote(pieces(count), pieces(count), ag_snd, came, me_c).wait_recv()

    def shift(hop, part):
        early = 3 * rows // 8
        at = pl.ds(0, early) if part == 0 else pl.ds(early, rows - early)
        if hop == 0:
            return remote(up_ref.at[at], relay.at[at], rl_snd, rl_rcv.at[part], None, relay_to)
        return remote(relay.at[at], up_v.at[at], up_snd, up_rcv, None, shift_to)

    def shift_start(hop, part):
        if n_pipe == 1:
            if (hop, part) == (0, 0):
                pltpu.make_async_copy(up_ref, up_v, up_rcv).start()
            return
        if hop == 1:
            shift(0, part).wait_recv()
        shift(hop, part).start()

    def chain(distance, upward):
        reach, to = (hp, ups) if upward else (hm, downs)
        zz = at_z(-distance if upward else distance)
        strides = {0: (1, 2, 4), 2: (1,), 4: (1, 2, 3, 4)}
        for stride in strides.get(distance, ()):
            if distance + stride <= reach:
                push(zz, lane, to[stride - 1], ag_z.at[int(upward), distance + stride - 1], own=distance == 0)

    chain(0, True)
    chain(0, False)
    push(z, lane, me_y, ag_y.at[0], own=True)
    push(z, lane, me_c, ag_c.at[0], own=True)

    with jax.named_scope("norm"):
        loads[0].wait()
        z_wide = z_v[...].astype(F32)
        factor = lax.rsqrt(jnp.mean(z_wide * z_wide, axis=-1, keepdims=True) + EPSILON)
        fac[...] = jnp.broadcast_to(factor, fac.shape)
        nb[...] = (z_wide * factor).astype(BF16)
        for k in range(zs):
            block = nb[:, k * width:(k + 1) * width].astype(F32)
            nt[k] = block.T.astype(BF16).reshape(LANES, feats, rows)

    def give(ll, to):
        remote(nt.at[:, ll], nt_sh.at[lane], nt_snd, nt_rcv, to).start()
    give(lane_d, me_d)
    give(lane_c, me_c)
    nt_sh[lane] = nt[:, lane]
    loads[1].wait()
    acc[...] = jnp.zeros_like(acc)

    def project(zz):
        at = pl.multiple_of(zz * width, width)
        acc[...] += dot(nb[:, pl.ds(at, width)], w_v[pl.ds(at, width), :])

    def slices(s):
        if s == 0:
            return [z]
        return ([at_z(-s)] if s <= hp else []) + ([at_z(s)] if s <= hm else [])

    order = [d for d in (1, 2, 4, 3, 5, 6, 7, 8) if d <= hp]
    assert len(order) == hp
    y_lag, c_lag = 7, 8

    def cross(s):
        found = slices(s)
        if s == order[-1]:
            arrive(2 * len(found), ag_y.at[s])
            return
        arrive(len(found), ag_y.at[s])
        for zz in found:
            push(zz, lane_y, me_c, ag_c.at[s])

    order = [0] + order
    for i in range(1, hp + c_lag + 1):
        with jax.named_scope(f"ag{i}"):
            if i <= hp:
                s = order[i]
                for zz, upward in zip(slices(s), (True, False)):
                    arrive(1, ag_z.at[int(upward), s - 1])
                    chain(s, upward)
                    push(zz, lane, me_y, ag_y.at[s])
                    if i == hp:
                        push(zz, lane, me_d, ag_y.at[s])
                    push(zz, lane, me_c, ag_c.at[s])
                if i == hp:
                    give(lane_y, me_y)
                    shift_start(0, 0)
                for back in range(max(0, i - y_lag), hp + 1) if i == hp else [i - y_lag]:
                    if back >= 0:
                        cross(order[back])
            if i >= c_lag:
                s = order[i - c_lag]
                found = slices(s)
                arrive((1 if s == order[-1] else 2) * len(found), ag_c.at[s])
                for zz in found:
                    project(zz)

    def halo_copies(group):
        own = kvw.at[group, 1]
        return (
            remote(own, kvw.at[group, 0], halo_snd, halo_rcv.at[group], right),
            remote(own, kvw.at[group, 2], halo_snd, halo_rcv.at[group], left),
        )

    for group in range(KV_HEADS):
        at_k, at_v = group * HEAD_DIM, (KV_HEADS + group) * HEAD_DIM
        kvw[group, 1, 0] = acc[:, at_k:at_k + HEAD_DIM].astype(BF16)
        kvw[group, 1, 1] = acc[:, at_v:at_v + HEAD_DIM].astype(BF16)
        for copy in halo_copies(group):
            copy.start()
    loads[2].wait()
    loads[3].wait()

    def halo_wait(group):
        both = kvw.at[group, pl.ds(0, 2)]
        remote(both, both, halo_snd, halo_rcv.at[group], right).wait_recv()

    key_pos = lax.broadcasted_iota(jnp.int32, (rows, rows), 0)
    query_pos = lax.broadcasted_iota(jnp.int32, (rows, rows), 1)
    lower = key_pos >= query_pos
    upper = key_pos <= query_pos

    def attention(group, heads):
        keys = kvw[group, :, 0].reshape(3 * rows, HEAD_DIM)
        values = kvw[group, :, 1].reshape(3 * rows, HEAD_DIM)
        parts = [slice(b * rows, (b + 1) * rows) for b in range(3)]

        def lanes(h):
            return slice((group * PER_GROUP + h) * HEAD_DIM, (group * PER_GROUP + h + 1) * HEAD_DIM)

        def multiply(h):
            slot = h % 2
            scores = dot(keys, q_v[:, lanes(h)], NT)
            s_buf[slot, parts[0]] = jnp.where(lower, scores[parts[0]], -1e30)
            s_buf[slot, parts[1]] = scores[parts[1]]
            s_buf[slot, parts[2]] = jnp.where(upper, scores[parts[2]], -1e30)
            d_buf[slot] = dot(values, g_v[:, lanes(h)], NT)

        def weigh(h):
            slot, into = h % 2, slice(h * HEAD_DIM, (h + 1) * HEAD_DIM)
            peak = jnp.maximum(jnp.maximum(s_buf[slot, parts[0]], s_buf[slot, parts[1]]), s_buf[slot, parts[2]])
            peak = over_keys(jnp.maximum, jnp.max, peak)
            total = row_dot = None
            for part in parts:
                lifted = jnp.exp2((s_buf[slot, part] - peak) * (scale * math.log2(math.e)))
                s_buf[slot, part] = lifted
                product = lifted * d_buf[slot, part]
                total = lifted if total is None else total + lifted
                row_dot = product if row_dot is None else row_dot + product
            inverse = 1.0 / over_keys(jnp.add, jnp.sum, total)
            row_dot = over_keys(jnp.add, jnp.sum, row_dot) * inverse
            for part in parts:
                lifted = s_buf[slot, part]
                p_all[part, into] = (lifted * inverse).astype(BF16)
                d_all[part, into] = (lifted * (inverse * scale) * (d_buf[slot, part] - row_dot)).astype(BF16)

        def spread_query(h):
            into = slice(h * HEAD_DIM, (h + 1) * HEAD_DIM)
            d_query = dot(d_all[:, into], keys, (((0,), (0,)), ((), ())))
            dq_v[:, lanes(h)] = d_query.astype(BF16)

        def sum_heads(first, last):
            into = slice(first * HEAD_DIM, last * HEAD_DIM)
            for ref, source, at in ((d_all, q_v, 0), (p_all, g_v, HEAD_DIM)):
                rest = jnp.concatenate([source[:, lanes(h)] for h in range(first, last)], axis=0)
                total = dot(ref[:, into], rest)
                if first > 0:
                    total = total + dkw[group, :, at:at + HEAD_DIM]
                dkw[group, :, at:at + HEAD_DIM] = total

        half = PER_GROUP // 2
        multiply(heads[0])
        for h in heads:
            if h != heads[-1]:
                multiply(h + 1)
            weigh(h)
            if h != heads[0]:
                spread_query(h - 1)
            if h == half:
                sum_heads(0, half)
        spread_query(heads[-1])
        if heads[-1] == PER_GROUP - 1:
            sum_heads(half, PER_GROUP)

    def fold_start(group):
        for side, start, to in ((0, 2 * rows, right), (1, 0, left)):
            folded[group, side] = dkw[group, start:start + rows].astype(BF16)
            remote(
                folded.at[group, side], fold.at[group, side], fold_snd, fold_rcv.at[group], to
            ).start()

    def share_start(group):
        remote(fold.at[group], fold.at[group], fold_snd, fold_rcv.at[group], right).wait_recv()
        total = dkw[group, rows:2 * rows] + fold[group, 0].astype(F32) + fold[group, 1].astype(F32)
        high = total.astype(BF16)
        low = (total - high.astype(F32)).astype(BF16)
        dkv_sh[lane, group] = high
        at_k, at_v = group * HEAD_DIM, (KV_HEADS + group) * HEAD_DIM
        for into, part in ((dkv_hi, high), (dkv_lo, low)):
            into[:, at_k:at_k + HEAD_DIM] = part[:, :HEAD_DIM]
            into[:, at_v:at_v + HEAD_DIM] = part[:, HEAD_DIM:]
        for kind, to in enumerate((me_y, me_c)):
            share(group, lane, kind, to).start()

    def share(group, ll, kind, to):
        part = dkv_sh.at[ll, group]
        return remote(part, part, sh_snd, sh_rcv.at[group, kind], to)

    def share_pass(group):
        share(group, lane_y, 0, me_c).wait_recv()
        share(group, lane_y, 1, me_c).start()

    def ring_refs(upward):
        if upward:
            return p_snd, p_rcv, p_sent, p_came, ups, hp
        return m_snd, m_rcv, m_sent, m_came, downs, hm

    def relayed(k):
        return k == 3 and REACH > 3

    def ring_slot(k):
        return {3: 3, 4: 2}.get(k, k - 1) if REACH > 3 else k - 1

    def ring_send(group, k, upward, total):
        snd, rcv, s_sem, r_sem, to, reach = ring_refs(upward)
        slot = k - 1 if reach < 4 else ring_slot(k)
        kind, step = (2, 1) if relayed(k) else (1, k - REACH) if k > REACH else (0, k)
        snd[group, slot] = total.astype(BF16)
        remote(
            snd.at[group, slot], rcv.at[group, slot], s_sem, r_sem.at[group, kind], to[step - 1]
        ).start()

    def ring_wait(group, upward, first, count, kind):
        _, rcv, s_sem, r_sem, to, _ = ring_refs(upward)
        some = rcv.at[group, pl.ds(first, count)]
        remote(some, some, s_sem, r_sem.at[group, kind], to[0]).wait_recv()
        return [rcv[group, first + k].astype(F32) for k in range(count)]

    def ring_start(group):
        two = dkv_sh.at[pl.ds(0, 2), group]
        remote(two, two, sh_snd, sh_rcv.at[group, 1], me_c).wait_recv()
        held = jnp.concatenate(
            [nt_sh[p].reshape(zs * feats, rows) for p in range(LANES)], axis=1
        )
        terms = dot(held, dkv_sh[:, group].reshape(LANES * rows, 2 * HEAD_DIM))
        prod[group] = terms.reshape(zs, feats, 2 * HEAD_DIM)
        for k in range(hp, REACH, -1):
            ring_both(group, k)

    def ring_both(group, k):
        for upward, reach in ((True, hp), (False, hm)):
            if k <= reach and (k != REACH or reach <= REACH):
                ring_send(group, k, upward, prod[group, at_z(k if upward else -k)])

    def ring_near(group):
        for k in range(min(REACH, hp), 0, -1):
            if k != 2:
                ring_both(group, k)

    def ring_next(group):
        for upward, reach in ((True, hp), (False, hm)):
            if reach >= 2 and REACH >= 2:
                total = prod[group, at_z(2 if upward else -2)]
                if reach >= 3 and REACH > 3:
                    (term,) = ring_wait(group, upward, 2 if reach < 4 else 3, 1, 2)
                    total = total + term
                ring_send(group, 2, upward, total)

    def ring_middle(group):
        for upward, reach in ((True, hp), (False, hm)):
            if reach > REACH:
                total = prod[group, at_z(REACH if upward else -REACH)]
                for term in ring_wait(group, upward, REACH, reach - REACH, 1):
                    total = total + term
                ring_send(group, REACH, upward, total)

    def ring_end(group):
        total = prod[group, z]
        for upward, reach in ((True, hp), (False, hm)):
            if reach > 0:
                near = min(REACH, reach)
                for term in ring_wait(group, upward, 0, near - int(near >= 3 and REACH > 3), 0):
                    total = total + term
        total = total * (1.0 / math.sqrt(rows * n_ctx))
        at_k, at_v = group * HEAD_DIM, (KV_HEADS + group) * HEAD_DIM
        wg_v[:, at_k:at_k + HEAD_DIM] = total[:, :HEAD_DIM]
        wg_v[:, at_v:at_v + HEAD_DIM] = total[:, HEAD_DIM:]

    with jax.named_scope("halo0"):
        halo_wait(0)
    with jax.named_scope("att0"):
        attention(0, range(PER_GROUP))
    fold_start(0)
    with jax.named_scope("halo1"):
        halo_wait(1)
    with jax.named_scope("att1"):
        attention(1, range(PER_GROUP))
    fold_start(1)
    with jax.named_scope("share0"):
        share_start(0)
    with jax.named_scope("nt"):
        three = nt_sh.at[pl.ds(0, LANES - 1)]
        remote(three, three, nt_snd, nt_rcv, me_c).wait_recv()
    with jax.named_scope("share1"):
        share_start(1)
    with jax.named_scope("pass0"):
        share_pass(0)
    shift_start(1, 0)
    shift_start(0, 1)
    with jax.named_scope("ring0"):
        ring_start(0)

    model = z_v.shape[1]
    blocks = 8
    span = model // blocks
    dot_sum[...] = jnp.zeros_like(dot_sum)

    def spread(b):
        w_b = w_v[b * span:(b + 1) * span, :]
        d_b = dot(dkv_hi[...], w_b, NT) + dot(dkv_lo[...], w_b, NT)
        dn[:, b * span:(b + 1) * span] = d_b
        normed = z_v[:, b * span:(b + 1) * span].astype(F32) * fac[:, :1]
        part = d_b * normed
        total = part[:, :128]
        for k in range(1, span // 128):
            total = total + part[:, k * 128:(k + 1) * 128]
        dot_sum[...] += total

    def finish(b, mean):
        at = slice(b * span, (b + 1) * span)
        normed = z_v[:, at].astype(F32) * fac[:, :1]
        branch = fac[:, :1] * (dn[:, at] - normed * mean)
        go_v[:, at] = (up_v[:, at].astype(F32) + branch).astype(BF16)

    todo = [functools.partial(spread, b) for b in range(blocks)]

    def last():
        with jax.named_scope("up"):
            if n_pipe > 1:
                remote(relay, up_v, up_snd, up_rcv, None, shift_to).wait_recv()
            else:
                pltpu.make_async_copy(up_ref, up_v, up_rcv).wait()
        mean = jnp.sum(dot_sum[...], axis=-1, keepdims=True) * (1.0 / model)
        for b in range(blocks):
            finish(b, mean)

    todo.append(last)
    def fill(count):
        for _ in range(count):
            if todo:
                todo.pop(0)()

    def stage(name, act):
        with jax.named_scope(name):
            act()

    stage("pass1", lambda: share_pass(1))
    stage("fill0", lambda: fill(3))
    stage("ring1", lambda: ring_start(1))
    stage("fill1", lambda: fill(2))
    stage("near", lambda: (ring_near(0), ring_near(1)))
    stage("mid0", lambda: ring_middle(0))
    stage("fwd", lambda: shift_start(1, 1))
    stage("fill2", lambda: fill(2))
    stage("mid1", lambda: ring_middle(1))
    stage("next", lambda: (ring_next(0), ring_next(1)))
    stage("end0", lambda: ring_end(0))
    stage("last", lambda: fill(len(todo)))
    stage("end1", lambda: ring_end(1))

    with jax.named_scope("drain"):
        all_sent = [
            (pieces(sent[0]), ag_snd), (nt.at[:, pl.ds(0, LANES - 1)], nt_snd),
            (kvw.at[:, pl.ds(0, 2)], halo_snd), (fold, fold_snd),
            (dkv_sh.at[pl.ds(0, LANES - 1)], sh_snd), (p_snd, p_sent),
        ]
        if hm > 0:
            all_sent.append((m_snd, m_sent))
        if n_pipe > 1:
            all_sent += [(up_v, up_snd), (relay, rl_snd)]
        for ref, sem in all_sent:
            remote(ref, ref, sem, sem, me_c).wait_send()


def store(go_v, dq_v, wg_v, go_ref, dq_ref, wg_ref, sem):
    copies = [
        pltpu.make_async_copy(src, dst, sem.at[i])
        for i, (src, dst) in enumerate(((go_v, go_ref), (dq_v, dq_ref), (wg_v, wg_ref)))
    ]
    for copy in copies:
        copy.start()
    for copy in copies:
        copy.wait()


def per_device(n_pipe, n_ctx, saved_in, grad_in, queries, d_heads, kv_weights):
    rows, model = saved_in.shape[1:]
    feats, kv_all = kv_weights.shape[1:]
    zs = n_ctx // LANES
    hp = zs // 2
    hm = max(1, zs - 1 - hp)
    pair = 2 * HEAD_DIM
    vm = pltpu.VMEM
    dma = pltpu.SemaphoreType.DMA
    big = vm((rows, model), BF16)
    scratch = [
        big, big, big, big, big,
        big, vm((rows, 128), F32),
        vm((zs, LANES, feats, rows), BF16), vm((LANES, zs, feats, rows), BF16),
        vm((n_ctx * feats, kv_all), BF16), vm((KV_HEADS, 3, 2, rows, HEAD_DIM), BF16), vm((rows, kv_all), F32),
        vm((KV_HEADS, 3 * rows, pair), F32), vm((KV_HEADS, 2, rows, pair), BF16), vm((KV_HEADS, 2, rows, pair), BF16),
        vm((rows, kv_all), BF16), vm((rows, kv_all), BF16),
        vm((LANES, KV_HEADS, rows, pair), BF16), vm((KV_HEADS, zs, feats, pair), F32),
        vm((rows, model), F32), vm((rows, 128), F32),
        vm((KV_HEADS, hp, feats, pair), BF16), vm((KV_HEADS, hp, feats, pair), BF16),
        vm((KV_HEADS, hm, feats, pair), BF16), vm((KV_HEADS, hm, feats, pair), BF16),
        vm((2, 3 * rows, HEAD_DIM), F32), vm((2, 3 * rows, HEAD_DIM), F32),
        vm((3 * rows, PER_GROUP * HEAD_DIM), BF16), vm((3 * rows, PER_GROUP * HEAD_DIM), BF16),
        dma((4,)), dma, dma((2, hp)), dma((hp + 1,)), dma((hp + 1,)),
        dma, dma, dma, dma, dma, dma((2,)),
        dma, dma((KV_HEADS,)), dma, dma((KV_HEADS,)),
        dma, dma((KV_HEADS, 2)),
        dma, dma((KV_HEADS, 3)), dma, dma((KV_HEADS, 3)),
    ]
    hbm = pl.BlockSpec(memory_space=pltpu.HBM)
    vmem = pl.BlockSpec(memory_space=pltpu.VMEM)
    shapes = (
        jax.ShapeDtypeStruct((rows, model), BF16),
        jax.ShapeDtypeStruct((rows, model), BF16),
        jax.ShapeDtypeStruct((feats, kv_all), F32),
    )
    results = pl.pallas_call(
        functools.partial(kernel, n_pipe, n_ctx),
        out_shape=shapes,
        in_specs=[hbm] * 5,
        out_specs=(vmem,) * 3,
        scratch_shapes=scratch,
        compiler_params=pltpu.CompilerParams(
            collective_id=0, has_side_effects=True, vmem_limit_bytes=48 * 1024 * 1024
        ),
        name="step",
    )(*(
        pltpu.with_memory_space_constraint(x[0], pltpu.HBM)
        for x in (saved_in, grad_in, queries, d_heads, kv_weights)
    ))
    grad_out, d_queries, weight_grad = pl.pallas_call(
        store,
        out_shape=shapes,
        in_specs=[vmem] * 3,
        out_specs=(hbm,) * 3,
        scratch_shapes=[dma((3,))],
        name="store",
    )(*(pltpu.with_memory_space_constraint(x, pltpu.VMEM) for x in results))
    return grad_out[None], d_queries[None], weight_grad[None]


def solution(mesh):
    spec = P("pipe", "ctx", None)
    return jax.shard_map(
        functools.partial(per_device, mesh.shape["pipe"], mesh.shape["ctx"]),
        mesh=mesh, in_specs=(spec,) * 5, out_specs=(spec,) * 3, check_vma=False,
    )
```
